32 devices in a mesh: azim: 8 (over z, core), slab: 4 (over y, x).
Axes of the slice: x: 2, y: 2, z: 4, core: 2. Of those that a mesh axis runs over, the one named last changes fastest.
Arguments:
- owned_trace: bfloat16 [384, 125, 256], P(('azim', 'slab')), may hold values from -6 to 6
- plus_trace: bfloat16 [128, 125, 256], P(('azim', 'slab')), may hold values from -6 to 6
- schur: bfloat16 [128, 750, 750], P(('azim', 'slab')), may hold values from -0.21875 to 0.21875
- recover: bfloat16 [128, 625, 750], P(('azim', 'slab')), may hold values from -0.21875 to 0.21875
- face_refs: int32 [128, 4], P(('azim', 'slab')), may hold values from 0 to 47, as said below
- orient: int32 [128, 6], P(('azim', 'slab')), may hold values from 0 to 7
Outputs:
- applied_owned: bfloat16 [384, 125, 256], P(('azim', 'slab'))
- applied_plus: bfloat16 [128, 125, 256], P(('azim', 'slab'))
- interior: bfloat16 [128, 625, 256], P(('azim', 'slab'))
The draws below stay inside these ranges and needn't reach their ends.
Inputs may be any that keep to these rules, and one draw needn't show every extreme that they name: `face_refs`: each entry names a face of the element's own sector as o * 12 + q, with o the owner's slab index and q a slot below 12. Of one device's 4 * 4 entries at most 5 name one owner; in every sector one owner is named exactly 5 times by every device of the sector.
All inputs are finite; a program needn't handle non-finite values.
Results may differ from the reference program's by a relative error of at most 0.0052.
Values may be sent and summed in bfloat16 or wider, within the bound.
A program may use at most 64 MiB of HBM per device.

```python
import jax
import jax.numpy as jnp
from jax import lax

DEGREE = 4
VARS = 5
FACE_NODES = 25
FACE_DOF = 125
ELEM_TRACE = 750
INT_DOF = 625
ELEM_DEV = 4
NRHS = 256
SECTORS = 8
SLABS = 4
FACE_CAP = 12
REQ_CAP = 5
ELEMENTS = 128
OWNED = 384


def face_layout(key):
    base = jax.random.fold_in(key, 11)
    key_hot = jax.random.fold_in(base, 1)
    key_count = jax.random.fold_in(base, 2)
    key_shift = jax.random.fold_in(base, 3)
    key_perm = jax.random.fold_in(base, 4)
    key_slot = jax.random.fold_in(base, 5)
    refs_dev = 4 * ELEM_DEV
    hot_owner = jax.random.randint(key_hot, (SECTORS,), 0, SLABS)
    counts = jax.random.randint(key_count, (SECTORS, SLABS), FACE_CAP // 2, FACE_CAP + 1)
    counts = jnp.where(jnp.arange(SLABS)[None, :] == hot_owner[:, None], FACE_CAP, counts)
    position = jnp.arange(refs_dev)
    offsets = jax.random.randint(key_shift, (SECTORS, SLABS, 1), 0, SLABS - 1)
    others = (position[None, None, :] - REQ_CAP + offsets) % (SLABS - 1)
    hot_column = hot_owner[:, None, None]
    owner_list = jnp.where(position[None, None, :] < REQ_CAP, hot_column, (hot_column + 1 + others) % SLABS)
    scores = jax.random.randint(key_perm, (SECTORS, SLABS, refs_dev), 0, 1 << 20) * refs_dev + position
    shuffle = jnp.argsort(scores, axis=-1)
    owner_final = jnp.take_along_axis(owner_list, shuffle, axis=-1)
    count_table = jnp.broadcast_to(counts[:, None, :], (SECTORS, SLABS, SLABS))
    slot_limit = jnp.take_along_axis(count_table, owner_final, axis=-1)
    slot_draw = jax.random.randint(key_slot, (SECTORS, SLABS, refs_dev), 0, slot_limit)
    face_ids = owner_final * FACE_CAP + slot_draw
    return face_ids.reshape(SECTORS * SLABS * ELEM_DEV, 4).astype(jnp.int32)


def draw_face_refs(key, part):
    return face_layout(key)


def touch_ends(result, key, low, top_value):
    longest = result.shape.index(max(result.shape))
    spots = []
    for shift in (0, 1):
        where = [jax.random.randint(jax.random.fold_in(key, axis), (), 0, length) for axis, length in enumerate(result.shape)]
        where[longest] = (where[longest] + shift) % result.shape[longest]
        spots.append(tuple(where))
    return result.at[spots[0]].set(low).at[spots[1]].set(top_value)


def level_of(key, extent, cuts, smallest, high):
    loudness, own = 1.0, jax.random.fold_in(key, 6)
    for dim, parts in cuts:
        heights = jnp.exp(jax.random.uniform(jax.random.fold_in(own, dim), (parts,), jnp.float32, smallest / len(cuts), high / len(cuts)))
        loudness = loudness * jnp.repeat(heights, extent[dim] // parts).reshape([-1 if axis == dim else 1 for axis in range(len(extent))])
    return loudness


def noise(stream_key, dims, scale, limit, cuts=(), kind=jnp.bfloat16):
    factor_of = level_of(stream_key, dims, cuts, -0.22, 0.18) if cuts else 1.0
    values = jax.random.normal(stream_key, dims, jnp.float32) * scale * factor_of
    return jnp.minimum(jnp.maximum(values, -limit), limit).astype(kind)


def setup_inputs(seed: int = 0) -> dict:
    keys = jax.random.split(jax.random.key(seed), 7)
    return {
        "owned_trace": noise(keys[0], (OWNED, FACE_DOF, NRHS), 1.0, 6.0, ((0, 32),)),
        "plus_trace": noise(keys[1], (ELEMENTS, FACE_DOF, NRHS), 1.0, 6.0, ((0, 32),)),
        "schur": noise(keys[2], (ELEMENTS, ELEM_TRACE, ELEM_TRACE), ELEM_TRACE ** -0.5, 0.21875, ((0, 32),)),
        "recover": noise(keys[3], (ELEMENTS, INT_DOF, ELEM_TRACE), ELEM_TRACE ** -0.5, 0.21875, ((0, 32),)),
        "face_refs": draw_face_refs(jax.random.fold_in(keys[6], 71), 0),
        "orient": touch_ends(jax.random.randint(keys[5], (ELEMENTS, 6), 0, 8), jax.random.fold_in(keys[5], 1), 0, 7).astype(jnp.int32),
    }


def orient_tables(grid_side):
    node_ids = jnp.arange(grid_side * grid_side)
    row_ids = node_ids // grid_side
    col_ids = node_ids % grid_side
    tables = []
    for code_value in range(8):
        first_ids, second_ids = row_ids, col_ids
        if code_value & 1:
            first_ids, second_ids = second_ids, first_ids
        if code_value & 2:
            first_ids = grid_side - 1 - first_ids
        if code_value & 4:
            second_ids = grid_side - 1 - second_ids
        tables.append(first_ids * grid_side + second_ids)
    source_ids = jnp.stack(tables)
    return (source_ids[:, :, None] == node_ids[None, None, :]).astype(jnp.float32)


def reference(owned_trace, plus_trace, schur, recover, face_refs, orient):
    tables = orient_tables(DEGREE + 1)
    sector_elems = SLABS * ELEM_DEV
    sector_faces = SLABS * FACE_CAP
    plus_sec = plus_trace.reshape(SECTORS, sector_elems, FACE_DOF, NRHS)
    minus_sec = jnp.roll(plus_sec, 1, axis=0)
    pieces = (owned_trace.reshape(SECTORS, sector_faces, FACE_DOF, NRHS), plus_sec, minus_sec,
              schur.reshape(SECTORS, sector_elems, ELEM_TRACE, ELEM_TRACE),
              recover.reshape(SECTORS, sector_elems, INT_DOF, ELEM_TRACE),
              face_refs.reshape(SECTORS, sector_elems, 4), orient.reshape(SECTORS, sector_elems, 6))

    def one_sector(piece_set):
        owned, plus, minus, blocks, recovers, face_ids, codes = piece_set
        radial = owned[face_ids]
        stacked = jnp.concatenate([minus[:, None], plus[:, None], radial], axis=1).astype(jnp.float32)
        stacked = stacked.reshape(sector_elems, 6, VARS, FACE_NODES, NRHS)
        node_perms = tables[codes]
        local_trace = jnp.einsum('efnm,efvmr->efvnr', node_perms, stacked)
        local_trace = local_trace.reshape(sector_elems, ELEM_TRACE, NRHS)
        response = jnp.einsum('eij,ejr->eir', blocks.astype(jnp.float32), local_trace)
        response = lax.optimization_barrier(response.astype(jnp.bfloat16)).astype(jnp.float32)
        interior = jnp.einsum('eij,ejr->eir', recovers.astype(jnp.float32), local_trace).astype(jnp.bfloat16)
        returned = jnp.einsum('efnm,efvnr->efvmr', node_perms,
                              response.reshape(sector_elems, 6, VARS, FACE_NODES, NRHS))
        returned = returned.reshape(sector_elems, 6, FACE_DOF, NRHS)
        owned_sum = jax.ops.segment_sum(returned[:, 2:].reshape(sector_elems * 4, FACE_DOF, NRHS),
                                        face_ids.reshape(-1), num_segments=sector_faces)
        return owned_sum, returned[:, 1], returned[:, 0], interior

    owned_sum, own_plus, to_previous, interior = lax.map(one_sector, pieces)
    applied_owned = owned_sum.astype(jnp.bfloat16).reshape(OWNED, FACE_DOF, NRHS)
    applied_plus = (own_plus + jnp.roll(to_previous, -1, axis=0)).astype(jnp.bfloat16)
    applied_plus = applied_plus.reshape(ELEMENTS, FACE_DOF, NRHS)
    return applied_owned, applied_plus, interior.reshape(ELEMENTS, INT_DOF, NRHS)
```

```python
import functools

import jax
import jax.numpy as jnp
from jax import lax
from jax.experimental import pallas as pl
from jax.experimental.pallas import tpu as pltpu
from jax.sharding import PartitionSpec as P

DEGREE = 4
CHUNKS = 2
ROWS = 144
MESH = pl.DeviceIdType.MESH


def source_of(face_row, code):
    side = DEGREE + 1
    variable = (face_row * 41) >> 10
    node = face_row - side * side * variable
    first = (node * 13) >> 6
    second = node - side * first
    swap, flip_first, flip_second = code & 1, (code >> 1) & 1, (code >> 2) & 1
    new_first = first + swap * (second - first)
    new_second = second + swap * (first - second)
    new_first = new_first + flip_first * (side - 1 - 2 * new_first)
    new_second = new_second + flip_second * (side - 1 - 2 * new_second)
    return side * side * variable + side * new_first + new_second


def in_blocks(rows, body):
    whole = rows // ROWS

    @pl.loop(0, whole)
    def _(b):
        body(pl.ds(pl.multiple_of(b * ROWS, ROWS), ROWS))

    if rows % ROWS:
        body(pl.ds(whole * ROWS, rows % ROWS))


def by_element(raw, out):
    def move(rows):
        out[:, rows, :] = pltpu.einshape("red->erd", raw[rows])

    in_blocks(raw.shape[0], move)


def partner(place, k, count):
    bit, other = 1, place
    while bit < count:
        other = other + ((k // bit) % 2) * bit * (1 - 2 * ((place // bit) % 2))
        bit *= 2
    return other


def kernel(
    dims,
    refs_hbm, orient_hbm, owned_hbm, plus_hbm, schur_hbm, recover_hbm,
    owned_out, plus_out, inner_out,
    refs_sm, orient_sm, owned_v, plus_raw, minus_raw, schur_raw, recover_raw,
    plus_v, minus_v, schur_v, recover_v, inner_v,
    asked_sm, slots_sm, before_sm, last_sm, req_v, req_sm, perm_v, permt_v,
    send_g, recv_gs, send_r, recv_r,
    ret_0, ret_1, ret_k, from_next, local_v, local_32, resp_32, sums,
    load_sems, req_send, req_recv, table_sem,
    minus_sems, gs_send, gs_recv, rt_send, rt_recv, fn_send, fn_recv,
):
    slabs, sectors, per_pair, elems, cap, dof, columns = dims
    width = columns // CHUNKS
    ref_total = 4 * elems
    me_a, me_s = lax.axis_index("azim"), lax.axis_index("slab")
    next_a, prev_a = lax.rem(me_a + 1, sectors), lax.rem(me_a + sectors - 1, sectors)

    def peer(k):
        return (me_a, partner(me_s, k, slabs))

    loads = [
        pltpu.make_async_copy(src, dst, load_sems.at[n])
        for n, (src, dst) in enumerate(
            ((owned_hbm, owned_v), (plus_hbm, plus_raw), (schur_hbm, schur_raw), (recover_hbm, recover_raw),
             (refs_hbm, refs_sm), (orient_hbm, orient_sm))
        )
    ]

    barrier = pltpu.get_barrier_semaphore()

    @pl.loop(1, slabs)
    def _(k):
        pl.semaphore_signal(barrier, inc=1, device_id=peer(slabs - k), device_id_type=MESH)

    for other in (next_a, prev_a):
        pl.semaphore_signal(barrier, inc=1, device_id=(other, me_s), device_id_type=MESH)

    for n in (0, 4):
        loads[n].start()

    def request(k):
        return pltpu.make_async_remote_copy(
            src_ref=refs_hbm, dst_ref=asked_sm.at[k], send_sem=req_send.at[k],
            recv_sem=req_recv.at[k], device_id=peer(k), device_id_type=MESH)

    minus = pltpu.make_async_remote_copy(
        src_ref=plus_hbm, dst_ref=minus_raw, send_sem=minus_sems.at[0],
        recv_sem=minus_sems.at[1], device_id=(next_a, me_s), device_id_type=MESH)

    pl.semaphore_wait(barrier, slabs + 1)

    @pl.loop(1, slabs)
    def _(k):
        request(slabs - k).start()

    minus.start()
    for n in (5, 1, 2, 3):
        loads[n].start()

    def give(c, k):
        return pltpu.make_async_remote_copy(
            src_ref=send_g.at[c, k], dst_ref=recv_gs[c].at[k], send_sem=gs_send.at[c, k],
            recv_sem=gs_recv.at[c, k], device_id=peer(k), device_id_type=MESH)

    def give_back(c, k):
        return pltpu.make_async_remote_copy(
            src_ref=send_r.at[c, k], dst_ref=recv_r.at[c, k], send_sem=rt_send.at[c, k],
            recv_sem=rt_recv.at[c, k], device_id=peer(k), device_id_type=MESH)

    def to_previous(c):
        return pltpu.make_async_remote_copy(
            src_ref=ret_0.at[c], dst_ref=from_next.at[c], send_sem=fn_send.at[c],
            recv_sem=fn_recv.at[c], device_id=(prev_a, me_s), device_id_type=MESH)

    def cols(c):
        return pl.ds(c * width, width)

    def place_slot(k, read):
        slots = [jnp.int32(-1)] * per_pair
        count = jnp.int32(0)
        for i in range(ref_total):
            value = read(i) - me_s * cap
            mine = (value >= 0) & (value < cap)
            for q in range(min(i + 1, per_pair)):
                slots[q] = jnp.where(mine & (count == q), value, slots[q])
            count = count + mine.astype(jnp.int32)
        for q in range(per_pair):
            slots_sm[k * per_pair + q] = slots[q]

    def fill(c, k):
        for q in range(per_pair):
            slot = jnp.clip(slots_sm[k * per_pair + q], 0, cap - 1)
            send_g[c, k, q] = owned_v[slot, :, cols(c)]
        give(c, k).start()

    loads[0].wait()

    @pl.loop(1, slabs)
    def _(k):
        request(k).wait()
        place_slot(k, lambda i: asked_sm[k, i // 4, i % 4])
        fill(0, k)

    for c in range(1, CHUNKS):
        @pl.loop(1, slabs)
        def _(k):
            fill(c, k)

    loads[4].wait()
    place_slot(0, lambda i: refs_sm[i // 4, i % 4])
    for q in range(per_pair):
        slot = jnp.clip(slots_sm[q], 0, cap - 1)
        for c in range(CHUNKS):
            recv_gs[c][0, q] = owned_v[slot, :, cols(c)]

    @pl.loop(0, slabs * per_pair)
    def _(j):
        slot, before = slots_sm[j], jnp.int32(0)
        for i in range(slabs * per_pair):
            before = jnp.where((slots_sm[i] == slot) & (i < j), i + 1, before)
        before_sm[j] = before

    @pl.loop(0, cap)
    def _(slot):
        last = jnp.int32(0)
        for i in range(slabs * per_pair):
            last = jnp.where(slots_sm[i] == slot, i + 1, last)
        last_sm[slot] = last

    sub = lax.broadcasted_iota(jnp.int32, (ref_total, 128), 0)
    lane = lax.broadcasted_iota(jnp.int32, (ref_total, 128), 1)
    ref_c = jnp.zeros((ref_total, 128), jnp.int32)
    ref_r = jnp.full((ref_total, 128), slabs * cap, jnp.int32)
    for i in range(ref_total):
        value = refs_sm[i // 4, i % 4]
        ref_c = jnp.where(sub == i, value, ref_c)
        ref_r = jnp.where(lane == i, value, ref_r)
    owner_c = jnp.zeros((ref_total, 128), jnp.int32)
    owner_r = jnp.zeros((ref_total, 128), jnp.int32)
    for o in range(1, slabs + 1):
        owner_c = owner_c + (ref_c >= o * cap).astype(jnp.int32)
        owner_r = owner_r + (ref_r >= o * cap).astype(jnp.int32)
    ahead = jnp.where((owner_c == owner_r) & (lane < sub), 1.0, 0.0)
    rank = jnp.sum(ahead, axis=1, keepdims=True)
    shift = partner(owner_c, me_s, slabs)
    target = (shift * per_pair).astype(jnp.float32) + rank
    hit = target == lane.astype(jnp.float32)
    source = jnp.sum(jnp.where(hit, sub.astype(jnp.float32), 0.0), axis=0, keepdims=True)
    where_to = jnp.sum(jnp.where(lane == sub, target, 0.0), axis=0, keepdims=True)
    row = lax.broadcasted_iota(jnp.int32, (8, 128), 0)
    req_v[...] = jnp.where(row == 0, source, where_to).astype(jnp.int32)

    to_scalars = pltpu.make_async_copy(req_v, req_sm, table_sem)
    to_scalars.start()
    to_scalars.wait()

    loads[5].wait()
    down_rows = lax.broadcasted_iota(jnp.int32, (dof, dof), 0)
    across = lax.broadcasted_iota(jnp.int32, (dof, dof), 1)

    @pl.loop(0, elems)
    def _(e):
        for f in range(6):
            code = orient_sm[e, f]
            perm_v[e, f] = jnp.where(source_of(down_rows, code) == across, 1.0, 0.0).astype(jnp.bfloat16)
            permt_v[e, f] = jnp.where(source_of(across, code) == down_rows, 1.0, 0.0).astype(jnp.bfloat16)

    sums[0] = jnp.zeros_like(sums[0])
    loads[2].wait()
    by_element(schur_raw, schur_v)
    loads[1].wait()
    plus_v[...] = pltpu.einshape("red->erd", plus_raw[...])
    minus.wait()
    minus_v[...] = pltpu.einshape("red->erd", minus_raw[...])

    for c in range(CHUNKS):
        @pl.loop(1, slabs)
        def _(k):
            give(c, k).wait()

        @pl.loop(0, elems)
        def _(e):
            for f in range(6):
                if f == 0:
                    face = minus_v[e, :, cols(c)]
                elif f == 1:
                    face = plus_v[e, :, cols(c)]
                else:
                    place = jnp.clip(req_sm[1, e * 4 + f - 2], 0, slabs * per_pair - 1)
                    face = recv_gs[c][place // per_pair, place % per_pair]
                local_32[pl.ds(f * dof, dof), :] = jnp.dot(
                    perm_v[e, f], face, preferred_element_type=jnp.float32)
            local = local_32[...].astype(jnp.bfloat16)
            local_v[e, :, cols(c)] = local
            resp_32[...] = jnp.dot(schur_v[e], local, preferred_element_type=jnp.float32)
            for f in range(6):
                part = resp_32[pl.ds(f * dof, dof), :].astype(jnp.bfloat16)
                back = jnp.dot(permt_v[e, f], part, preferred_element_type=jnp.float32).astype(jnp.bfloat16)
                if f == 0:
                    ret_0[c, e] = back
                elif f == 1:
                    ret_1[c, e] = back
                else:
                    ret_k[c, e * 4 + f - 2] = back

        @pl.loop(1, slabs)
        def _(step):
            k = slabs - step
            for q in range(per_pair):
                origin = jnp.clip(req_sm[0, k * per_pair + q], 0, ref_total - 1)
                send_r[c, k, q] = ret_k[c, origin]
            give_back(c, k).start()

        to_previous(c).start()
        for q in range(per_pair):
            origin = jnp.clip(req_sm[0, q], 0, ref_total - 1)
            recv_r[c, 0, q] = ret_k[c, origin]

    loads[3].wait()
    by_element(recover_raw, recover_v)

    @pl.loop(0, elems)
    def _(e):
        inner_v[e] = jnp.dot(recover_v[e], local_v[e], preferred_element_type=jnp.float32).astype(jnp.bfloat16)

    def interleave(rows):
        inner_out[rows] = pltpu.einshape("erd->red", inner_v[:, rows, :])

    in_blocks(inner_v.shape[1], interleave)

    def add_from(c, k):
        for q in range(per_pair):
            j = k * per_pair + q
            before = jnp.clip(before_sm[j], 0, slabs * per_pair)
            sums[j + 1] = recv_r[c, k, q].astype(jnp.float32) + sums[before]

    for c in range(CHUNKS):
        add_from(c, 0)
        to_previous(c).wait()

        total = ret_1[c].astype(jnp.float32) + from_next[c].astype(jnp.float32)
        plus_out[:, :, cols(c)] = pltpu.einshape("erd->red", total.astype(jnp.bfloat16))

        @pl.loop(1, slabs)
        def _(k):
            give_back(c, k).wait()
            add_from(c, k)

        @pl.loop(0, cap)
        def _(slot):
            last = jnp.clip(last_sm[slot], 0, slabs * per_pair)
            owned_out[slot, :, cols(c)] = sums[last].astype(jnp.bfloat16)


def finish(a_in, b_in, c_in, a_out, b_out, c_out, sems):
    moves = [
        pltpu.make_async_copy(src, dst, sems.at[n])
        for n, (src, dst) in enumerate(((a_in, a_out), (b_in, b_out), (c_in, c_out)))
    ]
    for move in moves:
        move.start()
    for move in moves:
        move.wait()


def swap(array):
    return jnp.swapaxes(array, 0, 1)


def per_device(owned_trace, plus_trace, schur, recover, face_refs, orient):
    elems, trace = schur.shape[:2]
    dof, columns = plus_trace.shape[1:]
    inner = recover.shape[1]
    cap = owned_trace.shape[0]
    slabs, sectors = lax.axis_size("slab"), lax.axis_size("azim")
    per_pair = (4 * elems + slabs - 1) // slabs + 1
    width = columns // CHUNKS
    bf16, f32 = jnp.bfloat16, jnp.float32
    dma = pltpu.SemaphoreType.DMA
    arrivals = [pltpu.VMEM((slabs, per_pair, dof, width), bf16)] * CHUNKS
    exchange = pltpu.VMEM((CHUNKS, slabs, per_pair, dof, width), bf16)
    per_elem = pltpu.VMEM((CHUNKS, elems, dof, width), bf16)
    vmem = pl.BlockSpec(memory_space=pltpu.VMEM)
    hbm = pl.BlockSpec(memory_space=pltpu.HBM)
    outs = pl.pallas_call(
        functools.partial(kernel, (slabs, sectors, per_pair, elems, cap, dof, columns)),
        out_shape=(
            jax.ShapeDtypeStruct(owned_trace.shape, bf16),
            jax.ShapeDtypeStruct((dof, elems, columns), bf16),
            jax.ShapeDtypeStruct((inner, elems, columns), bf16),
        ),
        in_specs=[hbm] * 6,
        out_specs=(vmem, vmem, vmem),
        scratch_shapes=[
            pltpu.SMEM(face_refs.shape, jnp.int32),
            pltpu.SMEM(orient.shape, jnp.int32),
            pltpu.VMEM(owned_trace.shape, bf16),
            pltpu.VMEM((dof, elems, columns), bf16),
            pltpu.VMEM((dof, elems, columns), bf16),
            pltpu.VMEM((trace, elems, trace), bf16),
            pltpu.VMEM((inner, elems, trace), bf16),
            pltpu.VMEM(plus_trace.shape, bf16),
            pltpu.VMEM(plus_trace.shape, bf16),
            pltpu.VMEM(schur.shape, bf16),
            pltpu.VMEM(recover.shape, bf16),
            pltpu.VMEM((elems, inner, columns), bf16),
            pltpu.SMEM((slabs,) + face_refs.shape, jnp.int32),
            pltpu.SMEM((slabs * per_pair,), jnp.int32),
            pltpu.SMEM((slabs * per_pair,), jnp.int32),
            pltpu.SMEM((cap,), jnp.int32),
            pltpu.VMEM((8, 128), jnp.int32),
            pltpu.SMEM((8, 128), jnp.int32),
            pltpu.VMEM((elems, 6, dof, dof), bf16),
            pltpu.VMEM((elems, 6, dof, dof), bf16),
            exchange, arrivals, exchange, exchange,
            per_elem, per_elem,
            pltpu.VMEM((CHUNKS, 4 * elems, dof, width), bf16),
            per_elem,
            pltpu.VMEM((elems, trace, columns), bf16),
            pltpu.VMEM((trace, width), f32),
            pltpu.VMEM((trace, width), f32),
            pltpu.VMEM((slabs * per_pair + 1, dof, width), f32),
            dma((6,)), dma((slabs,)), dma((slabs,)), dma,
            dma((2,)),
            dma((CHUNKS, slabs)), dma((CHUNKS, slabs)),
            dma((CHUNKS, slabs)), dma((CHUNKS, slabs)),
            dma((CHUNKS,)), dma((CHUNKS,)),
        ],
        compiler_params=pltpu.CompilerParams(
            collective_id=0, has_side_effects=True, vmem_limit_bytes=42 * 1024 * 1024),
    )(*(
        pltpu.with_memory_space_constraint(x, pltpu.HBM)
        for x in (face_refs, orient, owned_trace, swap(plus_trace), swap(schur), swap(recover))))
    owned_out, plus_out, inner_out = pl.pallas_call(
        finish,
        out_shape=tuple(jax.ShapeDtypeStruct(out.shape, out.dtype) for out in outs),
        in_specs=[vmem] * 3,
        out_specs=(hbm,) * 3,
        scratch_shapes=[dma((3,))],
        compiler_params=pltpu.CompilerParams(vmem_limit_bytes=1024 * 1024),
    )(*outs)
    return owned_out, swap(plus_out), swap(inner_out)


def solution(mesh):
    placed = P(("azim", "slab"), None, None)
    table = P(("azim", "slab"), None)
    return jax.shard_map(
        per_device,
        mesh=mesh,
        in_specs=(placed, placed, placed, placed, table, table),
        out_specs=(placed, placed, placed),
        check_vma=False,
    )
```

```python
import functools

import jax
import jax.numpy as jnp
from jax import lax
from jax.experimental import pallas as pl
from jax.experimental.pallas import tpu as pltpu
from jax.sharding import PartitionSpec as P

DEGREE = 4
CHUNKS = 2
ROWS = 144
MESH = pl.DeviceIdType.MESH


def source_of(face_row, code):
    side = DEGREE + 1
    variable = (face_row * 41) >> 10
    node = face_row - side * side * variable
    first = (node * 13) >> 6
    second = node - side * first
    swap, flip_first, flip_second = code & 1, (code >> 1) & 1, (code >> 2) & 1
    new_first = first + swap * (second - first)
    new_second = second + swap * (first - second)
    new_first = new_first + flip_first * (side - 1 - 2 * new_first)
    new_second = new_second + flip_second * (side - 1 - 2 * new_second)
    return side * side * variable + side * new_first + new_second


def in_blocks(rows, body):
    whole = rows // ROWS

    @pl.loop(0, whole)
    def _(b):
        body(pl.ds(pl.multiple_of(b * ROWS, ROWS), ROWS))

    if rows % ROWS:
        body(pl.ds(whole * ROWS, rows % ROWS))


def by_element(raw, out):
    def move(rows):
        out[:, rows, :] = pltpu.einshape("red->erd", raw[rows])

    in_blocks(raw.shape[0], move)


def partner(place, k, count):
    bit, other = 1, place
    while bit < count:
        other = other + ((k // bit) % 2) * bit * (1 - 2 * ((place // bit) % 2))
        bit *= 2
    return other


def kernel(
    dims,
    refs_hbm, orient_hbm, owned_hbm, plus_hbm, schur_hbm, recover_hbm,
    owned_out, plus_out, inner_out,
    refs_sm, orient_sm, owned_v, plus_raw, minus_raw, schur_raw, recover_raw,
    plus_v, minus_v, schur_v, recover_v, inner_v,
    asked_sm, slots_sm, before_sm, last_sm, req_v, req_sm, perm_v, permt_v,
    send_g, recv_gs, send_r, recv_r,
    ret_0, ret_1, ret_k, from_next, local_v, local_32, resp_32, sums,
    load_sems, req_send, req_recv, table_sem,
    minus_sems, gs_send, gs_recv, rt_send, rt_recv, fn_send, fn_recv, prev_ready,
):
    slabs, sectors, per_pair, elems, cap, dof, columns = dims
    width = columns // CHUNKS
    ref_total = 4 * elems
    me_a, me_s = lax.axis_index("azim"), lax.axis_index("slab")
    next_a, prev_a = lax.rem(me_a + 1, sectors), lax.rem(me_a + sectors - 1, sectors)

    def peer(k):
        return (me_a, partner(me_s, k, slabs))

    loads = [
        pltpu.make_async_copy(src, dst, load_sems.at[n])
        for n, (src, dst) in enumerate(
            ((owned_hbm, owned_v), (plus_hbm, plus_raw), (schur_hbm, schur_raw), (recover_hbm, recover_raw),
             (refs_hbm, refs_sm), (orient_hbm, orient_sm))
        )
    ]

    barrier = pltpu.get_barrier_semaphore()

    @pl.loop(1, slabs)
    def _(k):
        pl.semaphore_signal(barrier, inc=1, device_id=peer(slabs - k), device_id_type=MESH)

    even = lax.rem(me_a, 2) == 0
    pl.semaphore_signal(barrier, inc=1, device_id=(prev_a, me_s), device_id_type=MESH)

    @pl.when(even)
    def _():
        pl.semaphore_signal(barrier, inc=1, device_id=(next_a, me_s), device_id_type=MESH)

    for n in (0, 4):
        loads[n].start()

    def request(k):
        return pltpu.make_async_remote_copy(
            src_ref=refs_hbm, dst_ref=asked_sm.at[k], send_sem=req_send.at[k],
            recv_sem=req_recv.at[k], device_id=peer(k), device_id_type=MESH)

    minus = pltpu.make_async_remote_copy(
        src_ref=plus_hbm, dst_ref=minus_raw, send_sem=minus_sems.at[0],
        recv_sem=minus_sems.at[1], device_id=(next_a, me_s), device_id_type=MESH)

    @pl.when(even)
    def _():
        pl.semaphore_wait(barrier, slabs)

    @pl.when(jnp.logical_not(even))
    def _():
        pl.semaphore_wait(barrier, slabs + 1)
        pl.semaphore_signal(prev_ready, inc=1, device_id=(next_a, me_s), device_id_type=MESH)

    @pl.loop(1, slabs)
    def _(k):
        request(slabs - k).start()

    minus.start()
    for n in (5, 1, 2, 3):
        loads[n].start()

    def give(c, k):
        return pltpu.make_async_remote_copy(
            src_ref=send_g.at[c, k], dst_ref=recv_gs[c].at[k], send_sem=gs_send.at[c, k],
            recv_sem=gs_recv.at[c, k], device_id=peer(k), device_id_type=MESH)

    def give_back(c, k):
        return pltpu.make_async_remote_copy(
            src_ref=send_r.at[c, k], dst_ref=recv_r.at[c, k], send_sem=rt_send.at[c, k],
            recv_sem=rt_recv.at[c, k], device_id=peer(k), device_id_type=MESH)

    def to_previous(c):
        return pltpu.make_async_remote_copy(
            src_ref=ret_0.at[c], dst_ref=from_next.at[c], send_sem=fn_send.at[c],
            recv_sem=fn_recv.at[c], device_id=(prev_a, me_s), device_id_type=MESH)

    def cols(c):
        return pl.ds(c * width, width)

    def place_slot(k, read):
        slots = [jnp.int32(-1)] * per_pair
        count = jnp.int32(0)
        for i in range(ref_total):
            value = read(i) - me_s * cap
            mine = (value >= 0) & (value < cap)
            for q in range(min(i + 1, per_pair)):
                slots[q] = jnp.where(mine & (count == q), value, slots[q])
            count = count + mine.astype(jnp.int32)
        for q in range(per_pair):
            slots_sm[k * per_pair + q] = slots[q]

    def fill(c, k):
        for q in range(per_pair):
            slot = jnp.clip(slots_sm[k * per_pair + q], 0, cap - 1)
            send_g[c, k, q] = owned_v[slot, :, cols(c)]
        give(c, k).start()

    loads[0].wait()

    @pl.loop(1, slabs)
    def _(k):
        request(k).wait()
        place_slot(k, lambda i: asked_sm[k, i // 4, i % 4])
        fill(0, k)

    for c in range(1, CHUNKS):
        @pl.loop(1, slabs)
        def _(k):
            fill(c, k)

    loads[4].wait()
    place_slot(0, lambda i: refs_sm[i // 4, i % 4])
    for q in range(per_pair):
        slot = jnp.clip(slots_sm[q], 0, cap - 1)
        for c in range(CHUNKS):
            recv_gs[c][0, q] = owned_v[slot, :, cols(c)]

    @pl.loop(0, slabs * per_pair)
    def _(j):
        slot, before = slots_sm[j], jnp.int32(0)
        for i in range(slabs * per_pair):
            before = jnp.where((slots_sm[i] == slot) & (i < j), i + 1, before)
        before_sm[j] = before

    @pl.loop(0, cap)
    def _(slot):
        last = jnp.int32(0)
        for i in range(slabs * per_pair):
            last = jnp.where(slots_sm[i] == slot, i + 1, last)
        last_sm[slot] = last

    sub = lax.broadcasted_iota(jnp.int32, (ref_total, 128), 0)
    lane = lax.broadcasted_iota(jnp.int32, (ref_total, 128), 1)
    ref_c = jnp.zeros((ref_total, 128), jnp.int32)
    ref_r = jnp.full((ref_total, 128), slabs * cap, jnp.int32)
    for i in range(ref_total):
        value = refs_sm[i // 4, i % 4]
        ref_c = jnp.where(sub == i, value, ref_c)
        ref_r = jnp.where(lane == i, value, ref_r)
    owner_c = jnp.zeros((ref_total, 128), jnp.int32)
    owner_r = jnp.zeros((ref_total, 128), jnp.int32)
    for o in range(1, slabs + 1):
        owner_c = owner_c + (ref_c >= o * cap).astype(jnp.int32)
        owner_r = owner_r + (ref_r >= o * cap).astype(jnp.int32)
    ahead = jnp.where((owner_c == owner_r) & (lane < sub), 1.0, 0.0)
    rank = jnp.sum(ahead, axis=1, keepdims=True)
    shift = partner(owner_c, me_s, slabs)
    target = (shift * per_pair).astype(jnp.float32) + rank
    hit = target == lane.astype(jnp.float32)
    source = jnp.sum(jnp.where(hit, sub.astype(jnp.float32), 0.0), axis=0, keepdims=True)
    where_to = jnp.sum(jnp.where(lane == sub, target, 0.0), axis=0, keepdims=True)
    row = lax.broadcasted_iota(jnp.int32, (8, 128), 0)
    req_v[...] = jnp.where(row == 0, source, where_to).astype(jnp.int32)

    to_scalars = pltpu.make_async_copy(req_v, req_sm, table_sem)
    to_scalars.start()
    to_scalars.wait()

    loads[5].wait()
    down_rows = lax.broadcasted_iota(jnp.int32, (dof, dof), 0)
    across = lax.broadcasted_iota(jnp.int32, (dof, dof), 1)

    @pl.loop(0, elems)
    def _(e):
        for f in range(6):
            code = orient_sm[e, f]
            perm_v[e, f] = jnp.where(source_of(down_rows, code) == across, 1.0, 0.0).astype(jnp.bfloat16)
            permt_v[e, f] = jnp.where(source_of(across, code) == down_rows, 1.0, 0.0).astype(jnp.bfloat16)

    sums[0] = jnp.zeros_like(sums[0])
    loads[2].wait()
    by_element(schur_raw, schur_v)
    loads[1].wait()
    plus_v[...] = pltpu.einshape("red->erd", plus_raw[...])
    minus.wait()
    minus_v[...] = pltpu.einshape("red->erd", minus_raw[...])

    for c in range(CHUNKS):
        @pl.loop(1, slabs)
        def _(k):
            give(c, k).wait()

        @pl.loop(0, elems)
        def _(e):
            for f in range(6):
                if f == 0:
                    face = minus_v[e, :, cols(c)]
                elif f == 1:
                    face = plus_v[e, :, cols(c)]
                else:
                    place = jnp.clip(req_sm[1, e * 4 + f - 2], 0, slabs * per_pair - 1)
                    face = recv_gs[c][place // per_pair, place % per_pair]
                local_32[pl.ds(f * dof, dof), :] = jnp.dot(
                    perm_v[e, f], face, preferred_element_type=jnp.float32)
            local = local_32[...].astype(jnp.bfloat16)
            local_v[e, :, cols(c)] = local
            resp_32[...] = jnp.dot(schur_v[e], local, preferred_element_type=jnp.float32)
            for f in range(6):
                part = resp_32[pl.ds(f * dof, dof), :].astype(jnp.bfloat16)
                back = jnp.dot(permt_v[e, f], part, preferred_element_type=jnp.float32).astype(jnp.bfloat16)
                if f == 0:
                    ret_0[c, e] = back
                elif f == 1:
                    ret_1[c, e] = back
                else:
                    ret_k[c, e * 4 + f - 2] = back

        @pl.loop(1, slabs)
        def _(step):
            k = slabs - step
            for q in range(per_pair):
                origin = jnp.clip(req_sm[0, k * per_pair + q], 0, ref_total - 1)
                send_r[c, k, q] = ret_k[c, origin]
            give_back(c, k).start()

        if c == 0:
            @pl.when(even)
            def _():
                pl.semaphore_wait(prev_ready, 1)

        to_previous(c).start()
        for q in range(per_pair):
            origin = jnp.clip(req_sm[0, q], 0, ref_total - 1)
            recv_r[c, 0, q] = ret_k[c, origin]

    loads[3].wait()
    by_element(recover_raw, recover_v)

    @pl.loop(0, elems)
    def _(e):
        inner_v[e] = jnp.dot(recover_v[e], local_v[e], preferred_element_type=jnp.float32).astype(jnp.bfloat16)

    def interleave(rows):
        inner_out[rows] = pltpu.einshape("erd->red", inner_v[:, rows, :])

    in_blocks(inner_v.shape[1], interleave)

    def add_from(c, k):
        for q in range(per_pair):
            j = k * per_pair + q
            before = jnp.clip(before_sm[j], 0, slabs * per_pair)
            sums[j + 1] = recv_r[c, k, q].astype(jnp.float32) + sums[before]

    for c in range(CHUNKS):
        add_from(c, 0)
        to_previous(c).wait()

        total = ret_1[c].astype(jnp.float32) + from_next[c].astype(jnp.float32)
        plus_out[:, :, cols(c)] = pltpu.einshape("erd->red", total.astype(jnp.bfloat16))

        @pl.loop(1, slabs)
        def _(k):
            give_back(c, k).wait()
            add_from(c, k)

        @pl.loop(0, cap)
        def _(slot):
            last = jnp.clip(last_sm[slot], 0, slabs * per_pair)
            owned_out[slot, :, cols(c)] = sums[last].astype(jnp.bfloat16)


def finish(a_in, b_in, c_in, a_out, b_out, c_out, sems):
    moves = [
        pltpu.make_async_copy(src, dst, sems.at[n])
        for n, (src, dst) in enumerate(((a_in, a_out), (b_in, b_out), (c_in, c_out)))
    ]
    for move in moves:
        move.start()
    for move in moves:
        move.wait()


def swap(array):
    return jnp.swapaxes(array, 0, 1)


def per_device(owned_trace, plus_trace, schur, recover, face_refs, orient):
    elems, trace = schur.shape[:2]
    dof, columns = plus_trace.shape[1:]
    inner = recover.shape[1]
    cap = owned_trace.shape[0]
    slabs, sectors = lax.axis_size("slab"), lax.axis_size("azim")
    per_pair = (4 * elems + slabs - 1) // slabs + 1
    width = columns // CHUNKS
    bf16, f32 = jnp.bfloat16, jnp.float32
    dma = pltpu.SemaphoreType.DMA
    arrivals = [pltpu.VMEM((slabs, per_pair, dof, width), bf16)] * CHUNKS
    exchange = pltpu.VMEM((CHUNKS, slabs, per_pair, dof, width), bf16)
    per_elem = pltpu.VMEM((CHUNKS, elems, dof, width), bf16)
    vmem = pl.BlockSpec(memory_space=pltpu.VMEM)
    hbm = pl.BlockSpec(memory_space=pltpu.HBM)
    outs = pl.pallas_call(
        functools.partial(kernel, (slabs, sectors, per_pair, elems, cap, dof, columns)),
        out_shape=(
            jax.ShapeDtypeStruct(owned_trace.shape, bf16),
            jax.ShapeDtypeStruct((dof, elems, columns), bf16),
            jax.ShapeDtypeStruct((inner, elems, columns), bf16),
        ),
        in_specs=[hbm] * 6,
        out_specs=(vmem, vmem, vmem),
        scratch_shapes=[
            pltpu.SMEM(face_refs.shape, jnp.int32),
            pltpu.SMEM(orient.shape, jnp.int32),
            pltpu.VMEM(owned_trace.shape, bf16),
            pltpu.VMEM((dof, elems, columns), bf16),
            pltpu.VMEM((dof, elems, columns), bf16),
            pltpu.VMEM((trace, elems, trace), bf16),
            pltpu.VMEM((inner, elems, trace), bf16),
            pltpu.VMEM(plus_trace.shape, bf16),
            pltpu.VMEM(plus_trace.shape, bf16),
            pltpu.VMEM(schur.shape, bf16),
            pltpu.VMEM(recover.shape, bf16),
            pltpu.VMEM((elems, inner, columns), bf16),
            pltpu.SMEM((slabs,) + face_refs.shape, jnp.int32),
            pltpu.SMEM((slabs * per_pair,), jnp.int32),
            pltpu.SMEM((slabs * per_pair,), jnp.int32),
            pltpu.SMEM((cap,), jnp.int32),
            pltpu.VMEM((8, 128), jnp.int32),
            pltpu.SMEM((8, 128), jnp.int32),
            pltpu.VMEM((elems, 6, dof, dof), bf16),
            pltpu.VMEM((elems, 6, dof, dof), bf16),
            exchange, arrivals, exchange, exchange,
            per_elem, per_elem,
            pltpu.VMEM((CHUNKS, 4 * elems, dof, width), bf16),
            per_elem,
            pltpu.VMEM((elems, trace, columns), bf16),
            pltpu.VMEM((trace, width), f32),
            pltpu.VMEM((trace, width), f32),
            pltpu.VMEM((slabs * per_pair + 1, dof, width), f32),
            dma((6,)), dma((slabs,)), dma((slabs,)), dma,
            dma((2,)),
            dma((CHUNKS, slabs)), dma((CHUNKS, slabs)),
            dma((CHUNKS, slabs)), dma((CHUNKS, slabs)),
            dma((CHUNKS,)), dma((CHUNKS,)), pltpu.SemaphoreType.REGULAR,
        ],
        compiler_params=pltpu.CompilerParams(
            collective_id=0, has_side_effects=True, vmem_limit_bytes=42 * 1024 * 1024),
    )(*(
        pltpu.with_memory_space_constraint(x, pltpu.HBM)
        for x in (face_refs, orient, owned_trace, swap(plus_trace), swap(schur), swap(recover))))
    owned_out, plus_out, inner_out = pl.pallas_call(
        finish,
        out_shape=tuple(jax.ShapeDtypeStruct(out.shape, out.dtype) for out in outs),
        in_specs=[vmem] * 3,
        out_specs=(hbm,) * 3,
        scratch_shapes=[dma((3,))],
        compiler_params=pltpu.CompilerParams(vmem_limit_bytes=1024 * 1024),
    )(*outs)
    return owned_out, swap(plus_out), swap(inner_out)


def solution(mesh):
    placed = P(("azim", "slab"), None, None)
    table = P(("azim", "slab"), None)
    return jax.shard_map(
        per_device,
        mesh=mesh,
        in_specs=(placed, placed, placed, placed, table, table),
        out_specs=(placed, placed, placed),
        check_vma=False,
    )
```

```python
import functools

import jax
import jax.numpy as jnp
from jax import lax
from jax.experimental import pallas as pl
from jax.experimental.pallas import tpu as pltpu
from jax.sharding import PartitionSpec as P

DEGREE = 4
CHUNKS = 2
EARLY = 16
ROWS = 144
MESH = pl.DeviceIdType.MESH


def source_of(face_row, code):
    side = DEGREE + 1
    variable = (face_row * 41) >> 10
    node = face_row - side * side * variable
    first = (node * 13) >> 6
    second = node - side * first
    swap, flip_first, flip_second = code & 1, (code >> 1) & 1, (code >> 2) & 1
    new_first = first + swap * (second - first)
    new_second = second + swap * (first - second)
    new_first = new_first + flip_first * (side - 1 - 2 * new_first)
    new_second = new_second + flip_second * (side - 1 - 2 * new_second)
    return side * side * variable + side * new_first + new_second


def in_blocks(rows, body):
    whole = rows // ROWS

    @pl.loop(0, whole)
    def _(b):
        body(pl.ds(pl.multiple_of(b * ROWS, ROWS), ROWS))

    if rows % ROWS:
        body(pl.ds(whole * ROWS, rows % ROWS))


def by_element(raw, out):
    def move(rows):
        out[:, rows, :] = pltpu.einshape("red->erd", raw[rows])

    in_blocks(raw.shape[0], move)


def partner(place, k, count):
    bit, other = 1, place
    while bit < count:
        other = other + ((k // bit) % 2) * bit * (1 - 2 * ((place // bit) % 2))
        bit *= 2
    return other


def kernel(
    dims,
    refs_hbm, orient_hbm, owned_hbm, plus_hbm, schur_hbm, recover_hbm,
    owned_out, plus_out, inner_out,
    refs_sm, orient_sm, owned_v, plus_raw, minus_raw, schur_raw, recover_raw,
    plus_v, minus_v, schur_v, recover_v, inner_v,
    asked_sm, slots_sm, before_sm, last_sm, req_v, req_sm, perm_v, permt_v,
    send_gs, recv_gs, early_v, face_v, send_r, recv_r,
    ret_0, ret_1, ret_k, from_next, local_v, local_32, resp_32, sums,
    load_sems, req_send, req_recv, table_sem,
    minus_sems, early_send, early_recv, gs_send, gs_recv, rt_send, rt_recv, fn_send, fn_recv, prev_ready,
):
    slabs, sectors, per_pair, elems, cap, dof, columns = dims
    width = columns // CHUNKS
    ref_total = 4 * elems
    me_a, me_s = lax.axis_index("azim"), lax.axis_index("slab")
    next_a, prev_a = lax.rem(me_a + 1, sectors), lax.rem(me_a + sectors - 1, sectors)

    def peer(k):
        return (me_a, partner(me_s, k, slabs))

    loads = [
        pltpu.make_async_copy(src, dst, load_sems.at[n])
        for n, (src, dst) in enumerate(
            ((owned_hbm, owned_v), (plus_hbm, plus_raw), (schur_hbm, schur_raw), (recover_hbm, recover_raw),
             (refs_hbm, refs_sm), (orient_hbm, orient_sm))
        )
    ]

    barrier = pltpu.get_barrier_semaphore()

    @pl.loop(1, slabs)
    def _(k):
        pl.semaphore_signal(barrier, inc=1, device_id=peer(slabs - k), device_id_type=MESH)

    even = lax.rem(me_a, 2) == 0
    pl.semaphore_signal(barrier, inc=1, device_id=(prev_a, me_s), device_id_type=MESH)

    @pl.when(even)
    def _():
        pl.semaphore_signal(barrier, inc=1, device_id=(next_a, me_s), device_id_type=MESH)

    for n in (0, 4):
        loads[n].start()

    def request(k):
        return pltpu.make_async_remote_copy(
            src_ref=refs_hbm, dst_ref=asked_sm.at[k], send_sem=req_send.at[k],
            recv_sem=req_recv.at[k], device_id=peer(k), device_id_type=MESH)

    minus = pltpu.make_async_remote_copy(
        src_ref=plus_hbm, dst_ref=minus_raw, send_sem=minus_sems.at[0],
        recv_sem=minus_sems.at[1], device_id=(next_a, me_s), device_id_type=MESH)

    @pl.when(even)
    def _():
        pl.semaphore_wait(barrier, slabs)

    @pl.when(jnp.logical_not(even))
    def _():
        pl.semaphore_wait(barrier, slabs + 1)
        pl.semaphore_signal(prev_ready, inc=1, device_id=(next_a, me_s), device_id_type=MESH)

    @pl.loop(1, slabs)
    def _(k):
        request(slabs - k).start()

    def early(k):
        return pltpu.make_async_remote_copy(
            src_ref=owned_hbm.at[:, pl.ds(0, EARLY), pl.ds(0, width)], dst_ref=early_v.at[k],
            send_sem=early_send.at[k], recv_sem=early_recv.at[k], device_id=peer(k), device_id_type=MESH)

    @pl.loop(1, slabs)
    def _(k):
        early(slabs - k).start()

    minus.start()
    for n in (5, 1, 2, 3):
        loads[n].start()

    def give(c, k):
        return pltpu.make_async_remote_copy(
            src_ref=send_gs[c].at[k], dst_ref=recv_gs[c].at[k], send_sem=gs_send.at[c, k],
            recv_sem=gs_recv.at[c, k], device_id=peer(k), device_id_type=MESH)

    def give_back(c, k):
        return pltpu.make_async_remote_copy(
            src_ref=send_r.at[c, k], dst_ref=recv_r.at[c, k], send_sem=rt_send.at[c, k],
            recv_sem=rt_recv.at[c, k], device_id=peer(k), device_id_type=MESH)

    def to_previous(c):
        return pltpu.make_async_remote_copy(
            src_ref=ret_0.at[c], dst_ref=from_next.at[c], send_sem=fn_send.at[c],
            recv_sem=fn_recv.at[c], device_id=(prev_a, me_s), device_id_type=MESH)

    def cols(c):
        return pl.ds(c * width, width)

    def first_row(c):
        return EARLY if c == 0 else 0

    def place_slot(k, read):
        slots = [jnp.int32(-1)] * per_pair
        count = jnp.int32(0)
        for i in range(ref_total):
            value = read(i) - me_s * cap
            mine = (value >= 0) & (value < cap)
            for q in range(min(i + 1, per_pair)):
                slots[q] = jnp.where(mine & (count == q), value, slots[q])
            count = count + mine.astype(jnp.int32)
        for q in range(per_pair):
            slots_sm[k * per_pair + q] = slots[q]

    def fill(c, k):
        for q in range(per_pair):
            slot = jnp.clip(slots_sm[k * per_pair + q], 0, cap - 1)
            send_gs[c][k, q] = owned_v[slot, pl.ds(first_row(c), dof - first_row(c)), cols(c)]
        give(c, k).start()

    loads[0].wait()

    @pl.loop(1, slabs)
    def _(k):
        request(k).wait()
        place_slot(k, lambda i: asked_sm[k, i // 4, i % 4])
        fill(0, k)

    for c in range(1, CHUNKS):
        @pl.loop(1, slabs)
        def _(k):
            fill(c, k)

    early_v[0] = owned_v[:, pl.ds(0, EARLY), pl.ds(0, width)]
    loads[4].wait()
    place_slot(0, lambda i: refs_sm[i // 4, i % 4])
    for q in range(per_pair):
        slot = jnp.clip(slots_sm[q], 0, cap - 1)
        for c in range(CHUNKS):
            recv_gs[c][0, q] = owned_v[slot, pl.ds(first_row(c), dof - first_row(c)), cols(c)]

    @pl.loop(0, slabs * per_pair)
    def _(j):
        slot, before = slots_sm[j], jnp.int32(0)
        for i in range(slabs * per_pair):
            before = jnp.where((slots_sm[i] == slot) & (i < j), i + 1, before)
        before_sm[j] = before

    @pl.loop(0, cap)
    def _(slot):
        last = jnp.int32(0)
        for i in range(slabs * per_pair):
            last = jnp.where(slots_sm[i] == slot, i + 1, last)
        last_sm[slot] = last

    sub = lax.broadcasted_iota(jnp.int32, (ref_total, 128), 0)
    lane = lax.broadcasted_iota(jnp.int32, (ref_total, 128), 1)
    ref_c = jnp.zeros((ref_total, 128), jnp.int32)
    ref_r = jnp.full((ref_total, 128), slabs * cap, jnp.int32)
    for i in range(ref_total):
        value = refs_sm[i // 4, i % 4]
        ref_c = jnp.where(sub == i, value, ref_c)
        ref_r = jnp.where(lane == i, value, ref_r)
    owner_c = jnp.zeros((ref_total, 128), jnp.int32)
    owner_r = jnp.zeros((ref_total, 128), jnp.int32)
    for o in range(1, slabs + 1):
        owner_c = owner_c + (ref_c >= o * cap).astype(jnp.int32)
        owner_r = owner_r + (ref_r >= o * cap).astype(jnp.int32)
    ahead = jnp.where((owner_c == owner_r) & (lane < sub), 1.0, 0.0)
    rank = jnp.sum(ahead, axis=1, keepdims=True)
    shift = partner(owner_c, me_s, slabs)
    target = (shift * per_pair).astype(jnp.float32) + rank
    hit = target == lane.astype(jnp.float32)
    source = jnp.sum(jnp.where(hit, sub.astype(jnp.float32), 0.0), axis=0, keepdims=True)
    where_to = jnp.sum(jnp.where(lane == sub, target, 0.0), axis=0, keepdims=True)
    row = lax.broadcasted_iota(jnp.int32, (8, 128), 0)
    slot_of = jnp.sum(jnp.where(lane == sub, (ref_c - owner_c * cap).astype(jnp.float32), 0.0), axis=0, keepdims=True)
    req_v[...] = jnp.where(row == 0, source, jnp.where(row == 1, where_to, slot_of)).astype(jnp.int32)

    to_scalars = pltpu.make_async_copy(req_v, req_sm, table_sem)
    to_scalars.start()
    to_scalars.wait()

    loads[5].wait()
    down_rows = lax.broadcasted_iota(jnp.int32, (dof, dof), 0)
    across = lax.broadcasted_iota(jnp.int32, (dof, dof), 1)

    @pl.loop(0, elems)
    def _(e):
        for f in range(6):
            code = orient_sm[e, f]
            perm_v[e, f] = jnp.where(source_of(down_rows, code) == across, 1.0, 0.0).astype(jnp.bfloat16)
            permt_v[e, f] = jnp.where(source_of(across, code) == down_rows, 1.0, 0.0).astype(jnp.bfloat16)

    sums[0] = jnp.zeros_like(sums[0])
    loads[2].wait()
    by_element(schur_raw, schur_v)
    loads[1].wait()
    plus_v[...] = pltpu.einshape("red->erd", plus_raw[...])
    minus.wait()
    minus_v[...] = pltpu.einshape("red->erd", minus_raw[...])

    for c in range(CHUNKS):
        @pl.loop(1, slabs)
        def _(k):
            if c == 0:
                early(k).wait()
            give(c, k).wait()

        @pl.loop(0, elems)
        def _(e):
            for f in range(6):
                if f == 0:
                    face = minus_v[e, :, cols(c)]
                elif f == 1:
                    face = plus_v[e, :, cols(c)]
                else:
                    place = jnp.clip(req_sm[1, e * 4 + f - 2], 0, slabs * per_pair - 1)
                    if c == 0:
                        slot = jnp.clip(req_sm[2, e * 4 + f - 2], 0, cap - 1)
                        face_v[pl.ds(0, EARLY), :] = early_v[place // per_pair, slot]
                        face_v[pl.ds(EARLY, dof - EARLY), :] = recv_gs[c][place // per_pair, place % per_pair]
                        face = face_v[...]
                    else:
                        face = recv_gs[c][place // per_pair, place % per_pair]
                local_32[pl.ds(f * dof, dof), :] = jnp.dot(
                    perm_v[e, f], face, preferred_element_type=jnp.float32)
            local = local_32[...].astype(jnp.bfloat16)
            local_v[e, :, cols(c)] = local
            resp_32[...] = jnp.dot(schur_v[e], local, preferred_element_type=jnp.float32)
            for f in range(6):
                part = resp_32[pl.ds(f * dof, dof), :].astype(jnp.bfloat16)
                back = jnp.dot(permt_v[e, f], part, preferred_element_type=jnp.float32).astype(jnp.bfloat16)
                if f == 0:
                    ret_0[c, e] = back
                elif f == 1:
                    ret_1[c, e] = back
                else:
                    ret_k[c, e * 4 + f - 2] = back

        @pl.loop(1, slabs)
        def _(step):
            k = slabs - step
            for q in range(per_pair):
                origin = jnp.clip(req_sm[0, k * per_pair + q], 0, ref_total - 1)
                send_r[c, k, q] = ret_k[c, origin]
            give_back(c, k).start()

        if c == 0:
            @pl.when(even)
            def _():
                pl.semaphore_wait(prev_ready, 1)

        to_previous(c).start()
        for q in range(per_pair):
            origin = jnp.clip(req_sm[0, q], 0, ref_total - 1)
            recv_r[c, 0, q] = ret_k[c, origin]

    loads[3].wait()
    by_element(recover_raw, recover_v)

    @pl.loop(0, elems)
    def _(e):
        inner_v[e] = jnp.dot(recover_v[e], local_v[e], preferred_element_type=jnp.float32).astype(jnp.bfloat16)

    def interleave(rows):
        inner_out[rows] = pltpu.einshape("erd->red", inner_v[:, rows, :])

    in_blocks(inner_v.shape[1], interleave)

    def add_from(c, k):
        for q in range(per_pair):
            j = k * per_pair + q
            before = jnp.clip(before_sm[j], 0, slabs * per_pair)
            sums[j + 1] = recv_r[c, k, q].astype(jnp.float32) + sums[before]

    for c in range(CHUNKS):
        add_from(c, 0)
        to_previous(c).wait()

        total = ret_1[c].astype(jnp.float32) + from_next[c].astype(jnp.float32)
        plus_out[:, :, cols(c)] = pltpu.einshape("erd->red", total.astype(jnp.bfloat16))

        @pl.loop(1, slabs)
        def _(k):
            give_back(c, k).wait()
            add_from(c, k)

        @pl.loop(0, cap)
        def _(slot):
            last = jnp.clip(last_sm[slot], 0, slabs * per_pair)
            owned_out[slot, :, cols(c)] = sums[last].astype(jnp.bfloat16)


def finish(a_in, b_in, c_in, a_out, b_out, c_out, sems):
    moves = [
        pltpu.make_async_copy(src, dst, sems.at[n])
        for n, (src, dst) in enumerate(((a_in, a_out), (b_in, b_out), (c_in, c_out)))
    ]
    for move in moves:
        move.start()
    for move in moves:
        move.wait()


def swap(array):
    return jnp.swapaxes(array, 0, 1)


def per_device(owned_trace, plus_trace, schur, recover, face_refs, orient):
    elems, trace = schur.shape[:2]
    dof, columns = plus_trace.shape[1:]
    inner = recover.shape[1]
    cap = owned_trace.shape[0]
    slabs, sectors = lax.axis_size("slab"), lax.axis_size("azim")
    per_pair = (4 * elems + slabs - 1) // slabs + 1
    width = columns // CHUNKS
    bf16, f32 = jnp.bfloat16, jnp.float32
    dma = pltpu.SemaphoreType.DMA
    arrivals = [
        pltpu.VMEM((slabs, per_pair, dof - (EARLY if c == 0 else 0), width), bf16) for c in range(CHUNKS)]
    exchange = pltpu.VMEM((CHUNKS, slabs, per_pair, dof, width), bf16)
    per_elem = pltpu.VMEM((CHUNKS, elems, dof, width), bf16)
    vmem = pl.BlockSpec(memory_space=pltpu.VMEM)
    hbm = pl.BlockSpec(memory_space=pltpu.HBM)
    outs = pl.pallas_call(
        functools.partial(kernel, (slabs, sectors, per_pair, elems, cap, dof, columns)),
        out_shape=(
            jax.ShapeDtypeStruct(owned_trace.shape, bf16),
            jax.ShapeDtypeStruct((dof, elems, columns), bf16),
            jax.ShapeDtypeStruct((inner, elems, columns), bf16),
        ),
        in_specs=[hbm] * 6,
        out_specs=(vmem, vmem, vmem),
        scratch_shapes=[
            pltpu.SMEM(face_refs.shape, jnp.int32),
            pltpu.SMEM(orient.shape, jnp.int32),
            pltpu.VMEM(owned_trace.shape, bf16),
            pltpu.VMEM((dof, elems, columns), bf16),
            pltpu.VMEM((dof, elems, columns), bf16),
            pltpu.VMEM((trace, elems, trace), bf16),
            pltpu.VMEM((inner, elems, trace), bf16),
            pltpu.VMEM(plus_trace.shape, bf16),
            pltpu.VMEM(plus_trace.shape, bf16),
            pltpu.VMEM(schur.shape, bf16),
            pltpu.VMEM(recover.shape, bf16),
            pltpu.VMEM((elems, inner, columns), bf16),
            pltpu.SMEM((slabs,) + face_refs.shape, jnp.int32),
            pltpu.SMEM((slabs * per_pair,), jnp.int32),
            pltpu.SMEM((slabs * per_pair,), jnp.int32),
            pltpu.SMEM((cap,), jnp.int32),
            pltpu.VMEM((8, 128), jnp.int32),
            pltpu.SMEM((8, 128), jnp.int32),
            pltpu.VMEM((elems, 6, dof, dof), bf16),
            pltpu.VMEM((elems, 6, dof, dof), bf16),
            arrivals, arrivals,
            pltpu.VMEM((slabs, cap, EARLY, width), bf16),
            pltpu.VMEM((dof, width), bf16),
            exchange, exchange,
            per_elem, per_elem,
            pltpu.VMEM((CHUNKS, 4 * elems, dof, width), bf16),
            per_elem,
            pltpu.VMEM((elems, trace, columns), bf16),
            pltpu.VMEM((trace, width), f32),
            pltpu.VMEM((trace, width), f32),
            pltpu.VMEM((slabs * per_pair + 1, dof, width), f32),
            dma((6,)), dma((slabs,)), dma((slabs,)), dma,
            dma((2,)), dma((slabs,)), dma((slabs,)),
            dma((CHUNKS, slabs)), dma((CHUNKS, slabs)),
            dma((CHUNKS, slabs)), dma((CHUNKS, slabs)),
            dma((CHUNKS,)), dma((CHUNKS,)), pltpu.SemaphoreType.REGULAR,
        ],
        compiler_params=pltpu.CompilerParams(
            collective_id=0, has_side_effects=True, vmem_limit_bytes=42 * 1024 * 1024),
    )(*(
        pltpu.with_memory_space_constraint(x, pltpu.HBM)
        for x in (face_refs, orient, owned_trace, swap(plus_trace), swap(schur), swap(recover))))
    owned_out, plus_out, inner_out = pl.pallas_call(
        finish,
        out_shape=tuple(jax.ShapeDtypeStruct(out.shape, out.dtype) for out in outs),
        in_specs=[vmem] * 3,
        out_specs=(hbm,) * 3,
        scratch_shapes=[dma((3,))],
        compiler_params=pltpu.CompilerParams(vmem_limit_bytes=1024 * 1024),
    )(*outs)
    return owned_out, swap(plus_out), swap(inner_out)


def solution(mesh):
    placed = P(("azim", "slab"), None, None)
    table = P(("azim", "slab"), None)
    return jax.shard_map(
        per_device,
        mesh=mesh,
        in_specs=(placed, placed, placed, placed, table, table),
        out_specs=(placed, placed, placed),
        check_vma=False,
    )
```

```python
import functools

import jax
import jax.numpy as jnp
from jax import lax
from jax.experimental import pallas as pl
from jax.experimental.pallas import tpu as pltpu
from jax.sharding import PartitionSpec as P

DEGREE = 4
CHUNKS = 2
EARLY = 16
ROWS = 144
MESH = pl.DeviceIdType.MESH


def source_of(face_row, code):
    side = DEGREE + 1
    variable = (face_row * 41) >> 10
    node = face_row - side * side * variable
    first = (node * 13) >> 6
    second = node - side * first
    swap, flip_first, flip_second = code & 1, (code >> 1) & 1, (code >> 2) & 1
    new_first = first + swap * (second - first)
    new_second = second + swap * (first - second)
    new_first = new_first + flip_first * (side - 1 - 2 * new_first)
    new_second = new_second + flip_second * (side - 1 - 2 * new_second)
    return side * side * variable + side * new_first + new_second


def in_blocks(rows, body):
    whole = rows // ROWS

    @pl.loop(0, whole)
    def _(b):
        body(pl.ds(pl.multiple_of(b * ROWS, ROWS), ROWS))

    if rows % ROWS:
        body(pl.ds(whole * ROWS, rows % ROWS))


def by_element(raw, out):
    def move(rows):
        out[:, rows, :] = pltpu.einshape("red->erd", raw[rows])

    in_blocks(raw.shape[0], move)


def partner(place, k, count):
    bit, other = 1, place
    while bit < count:
        other = other + ((k // bit) % 2) * bit * (1 - 2 * ((place // bit) % 2))
        bit *= 2
    return other


def kernel(
    dims,
    refs_hbm, orient_hbm, owned_hbm, plus_hbm, schur_hbm, recover_hbm,
    owned_out, plus_out, inner_out,
    refs_sm, orient_sm, owned_v, plus_raw, minus_raw, schur_raw, recover_raw,
    plus_v, minus_v, schur_v, recover_v, inner_v,
    asked_sm, slots_sm, before_sm, last_sm, req_v, req_sm, perm_v, permt_v,
    send_gs, recv_gs, early_v, face_v, send_r, recv_r,
    ret_0, ret_1, ret_k, from_next, local_v, local_32, resp_32, sums,
    load_sems, req_send, req_recv, table_sem,
    minus_sems, early_send, early_recv, gs_send, gs_recv, rt_send, rt_recv, fn_send, fn_recv, ready,
):
    slabs, sectors, per_pair, elems, cap, dof, columns = dims
    width = columns // CHUNKS
    ref_total = 4 * elems
    me_a, me_s = lax.axis_index("azim"), lax.axis_index("slab")
    next_a, prev_a = lax.rem(me_a + 1, sectors), lax.rem(me_a + sectors - 1, sectors)

    def peer(k):
        return (me_a, partner(me_s, k, slabs))

    loads = [
        pltpu.make_async_copy(src, dst, load_sems.at[n])
        for n, (src, dst) in enumerate(
            ((owned_hbm, owned_v), (plus_hbm, plus_raw), (schur_hbm, schur_raw), (recover_hbm, recover_raw),
             (refs_hbm, refs_sm), (orient_hbm, orient_sm))
        )
    ]

    barrier = pltpu.get_barrier_semaphore()

    @pl.loop(1, slabs)
    def _(k):
        pl.semaphore_signal(barrier, inc=1, device_id=peer(slabs - k), device_id_type=MESH)

    even = lax.rem(me_a, 2) == 0
    odd = jnp.logical_not(even)
    beside, across_a = jnp.where(even, next_a, prev_a), jnp.where(even, prev_a, next_a)
    first = across_a > me_a
    second = jnp.logical_not(first)
    pl.semaphore_signal(barrier, inc=1, device_id=(beside, me_s), device_id_type=MESH)

    @pl.when(first)
    def _():
        pl.semaphore_signal(barrier, inc=1, device_id=(across_a, me_s), device_id_type=MESH)

    for n in (0, 4):
        loads[n].start()

    def request(k):
        return pltpu.make_async_remote_copy(
            src_ref=refs_hbm, dst_ref=asked_sm.at[k], send_sem=req_send.at[k],
            recv_sem=req_recv.at[k], device_id=peer(k), device_id_type=MESH)

    minus = pltpu.make_async_remote_copy(
        src_ref=plus_hbm, dst_ref=minus_raw, send_sem=minus_sems.at[0],
        recv_sem=minus_sems.at[1], device_id=(next_a, me_s), device_id_type=MESH)

    @pl.when(first)
    def _():
        pl.semaphore_wait(barrier, slabs)

    @pl.when(second)
    def _():
        pl.semaphore_wait(barrier, slabs + 1)
        pl.semaphore_signal(ready, inc=1, device_id=(across_a, me_s), device_id_type=MESH)

    @pl.loop(1, slabs)
    def _(k):
        request(k).start()

    def early(k):
        return pltpu.make_async_remote_copy(
            src_ref=owned_hbm.at[:, pl.ds(0, EARLY), pl.ds(0, width)], dst_ref=early_v.at[k],
            send_sem=early_send.at[k], recv_sem=early_recv.at[k], device_id=peer(k), device_id_type=MESH)

    @pl.loop(1, slabs)
    def _(k):
        early(slabs - k).start()

    @pl.when(jnp.logical_or(even, second))
    def _():
        minus.start()

    for n in (5, 1, 2, 3):
        loads[n].start()

    def give(c, k):
        return pltpu.make_async_remote_copy(
            src_ref=send_gs[c].at[k], dst_ref=recv_gs[c].at[k], send_sem=gs_send.at[c, k],
            recv_sem=gs_recv.at[c, k], device_id=peer(k), device_id_type=MESH)

    def give_back(c, k):
        return pltpu.make_async_remote_copy(
            src_ref=send_r.at[c, k], dst_ref=recv_r.at[c, k], send_sem=rt_send.at[c, k],
            recv_sem=rt_recv.at[c, k], device_id=peer(k), device_id_type=MESH)

    def to_previous(c):
        return pltpu.make_async_remote_copy(
            src_ref=ret_0.at[c], dst_ref=from_next.at[c], send_sem=fn_send.at[c],
            recv_sem=fn_recv.at[c], device_id=(prev_a, me_s), device_id_type=MESH)

    def cols(c):
        return pl.ds(c * width, width)

    def first_row(c):
        return EARLY if c == 0 else 0

    def place_slot(k, read):
        slots = [jnp.int32(-1)] * per_pair
        count = jnp.int32(0)
        for i in range(ref_total):
            value = read(i) - me_s * cap
            mine = (value >= 0) & (value < cap)
            for q in range(min(i + 1, per_pair)):
                slots[q] = jnp.where(mine & (count == q), value, slots[q])
            count = count + mine.astype(jnp.int32)
        for q in range(per_pair):
            slots_sm[k * per_pair + q] = slots[q]

    def fill(c, k):
        for q in range(per_pair):
            slot = jnp.clip(slots_sm[k * per_pair + q], 0, cap - 1)
            send_gs[c][k, q] = owned_v[slot, pl.ds(first_row(c), dof - first_row(c)), cols(c)]
        give(c, k).start()

    loads[0].wait()

    @pl.loop(1, slabs)
    def _(k):
        request(k).wait()
        place_slot(k, lambda i: asked_sm[k, i // 4, i % 4])
        fill(0, k)

    for c in range(1, CHUNKS):
        @pl.loop(1, slabs)
        def _(k):
            fill(c, k)

    @pl.when(jnp.logical_and(odd, first))
    def _():
        pl.semaphore_wait(ready, 1)
        minus.start()

    early_v[0] = owned_v[:, pl.ds(0, EARLY), pl.ds(0, width)]
    loads[4].wait()
    place_slot(0, lambda i: refs_sm[i // 4, i % 4])
    for q in range(per_pair):
        slot = jnp.clip(slots_sm[q], 0, cap - 1)
        for c in range(CHUNKS):
            recv_gs[c][0, q] = owned_v[slot, pl.ds(first_row(c), dof - first_row(c)), cols(c)]

    @pl.loop(0, slabs * per_pair)
    def _(j):
        slot, before = slots_sm[j], jnp.int32(0)
        for i in range(slabs * per_pair):
            before = jnp.where((slots_sm[i] == slot) & (i < j), i + 1, before)
        before_sm[j] = before

    @pl.loop(0, cap)
    def _(slot):
        last = jnp.int32(0)
        for i in range(slabs * per_pair):
            last = jnp.where(slots_sm[i] == slot, i + 1, last)
        last_sm[slot] = last

    sub = lax.broadcasted_iota(jnp.int32, (ref_total, 128), 0)
    lane = lax.broadcasted_iota(jnp.int32, (ref_total, 128), 1)
    ref_c = jnp.zeros((ref_total, 128), jnp.int32)
    ref_r = jnp.full((ref_total, 128), slabs * cap, jnp.int32)
    for i in range(ref_total):
        value = refs_sm[i // 4, i % 4]
        ref_c = jnp.where(sub == i, value, ref_c)
        ref_r = jnp.where(lane == i, value, ref_r)
    owner_c = jnp.zeros((ref_total, 128), jnp.int32)
    owner_r = jnp.zeros((ref_total, 128), jnp.int32)
    for o in range(1, slabs + 1):
        owner_c = owner_c + (ref_c >= o * cap).astype(jnp.int32)
        owner_r = owner_r + (ref_r >= o * cap).astype(jnp.int32)
    ahead = jnp.where((owner_c == owner_r) & (lane < sub), 1.0, 0.0)
    rank = jnp.sum(ahead, axis=1, keepdims=True)
    shift = partner(owner_c, me_s, slabs)
    target = (shift * per_pair).astype(jnp.float32) + rank
    hit = target == lane.astype(jnp.float32)
    source = jnp.sum(jnp.where(hit, sub.astype(jnp.float32), 0.0), axis=0, keepdims=True)
    where_to = jnp.sum(jnp.where(lane == sub, target, 0.0), axis=0, keepdims=True)
    row = lax.broadcasted_iota(jnp.int32, (8, 128), 0)
    slot_of = jnp.sum(jnp.where(lane == sub, (ref_c - owner_c * cap).astype(jnp.float32), 0.0), axis=0, keepdims=True)
    req_v[...] = jnp.where(row == 0, source, jnp.where(row == 1, where_to, slot_of)).astype(jnp.int32)

    to_scalars = pltpu.make_async_copy(req_v, req_sm, table_sem)
    to_scalars.start()
    to_scalars.wait()

    loads[5].wait()
    down_rows = lax.broadcasted_iota(jnp.int32, (dof, dof), 0)
    across = lax.broadcasted_iota(jnp.int32, (dof, dof), 1)

    @pl.loop(0, elems)
    def _(e):
        for f in range(6):
            code = orient_sm[e, f]
            perm_v[e, f] = jnp.where(source_of(down_rows, code) == across, 1.0, 0.0).astype(jnp.bfloat16)
            permt_v[e, f] = jnp.where(source_of(across, code) == down_rows, 1.0, 0.0).astype(jnp.bfloat16)

    sums[0] = jnp.zeros_like(sums[0])
    loads[2].wait()
    by_element(schur_raw, schur_v)
    loads[1].wait()
    plus_v[...] = pltpu.einshape("red->erd", plus_raw[...])
    minus.wait()
    minus_v[...] = pltpu.einshape("red->erd", minus_raw[...])

    for c in range(CHUNKS):
        @pl.loop(1, slabs)
        def _(k):
            if c == 0:
                early(k).wait()
            give(c, k).wait()

        @pl.loop(0, elems)
        def _(e):
            for f in range(6):
                if f == 0:
                    face = minus_v[e, :, cols(c)]
                elif f == 1:
                    face = plus_v[e, :, cols(c)]
                else:
                    place = jnp.clip(req_sm[1, e * 4 + f - 2], 0, slabs * per_pair - 1)
                    if c == 0:
                        slot = jnp.clip(req_sm[2, e * 4 + f - 2], 0, cap - 1)
                        face_v[pl.ds(0, EARLY), :] = early_v[place // per_pair, slot]
                        face_v[pl.ds(EARLY, dof - EARLY), :] = recv_gs[c][place // per_pair, place % per_pair]
                        face = face_v[...]
                    else:
                        face = recv_gs[c][place // per_pair, place % per_pair]
                local_32[pl.ds(f * dof, dof), :] = jnp.dot(
                    perm_v[e, f], face, preferred_element_type=jnp.float32)
            local = local_32[...].astype(jnp.bfloat16)
            local_v[e, :, cols(c)] = local
            resp_32[...] = jnp.dot(schur_v[e], local, preferred_element_type=jnp.float32)
            for f in range(6):
                part = resp_32[pl.ds(f * dof, dof), :].astype(jnp.bfloat16)
                back = jnp.dot(permt_v[e, f], part, preferred_element_type=jnp.float32).astype(jnp.bfloat16)
                if f == 0:
                    ret_0[c, e] = back
                elif f == 1:
                    ret_1[c, e] = back
                else:
                    ret_k[c, e * 4 + f - 2] = back

        @pl.loop(1, slabs)
        def _(step):
            k = slabs - step
            for q in range(per_pair):
                origin = jnp.clip(req_sm[0, k * per_pair + q], 0, ref_total - 1)
                send_r[c, k, q] = ret_k[c, origin]
            give_back(c, k).start()

        if c == 0:
            @pl.when(jnp.logical_and(even, first))
            def _():
                pl.semaphore_wait(ready, 1)

        to_previous(c).start()
        for q in range(per_pair):
            origin = jnp.clip(req_sm[0, q], 0, ref_total - 1)
            recv_r[c, 0, q] = ret_k[c, origin]

    loads[3].wait()
    by_element(recover_raw, recover_v)

    @pl.loop(0, elems)
    def _(e):
        inner_v[e] = jnp.dot(recover_v[e], local_v[e], preferred_element_type=jnp.float32).astype(jnp.bfloat16)

    def interleave(rows):
        inner_out[rows] = pltpu.einshape("erd->red", inner_v[:, rows, :])

    in_blocks(inner_v.shape[1], interleave)

    def add_from(c, k):
        for q in range(per_pair):
            j = k * per_pair + q
            before = jnp.clip(before_sm[j], 0, slabs * per_pair)
            sums[j + 1] = recv_r[c, k, q].astype(jnp.float32) + sums[before]

    for c in range(CHUNKS):
        add_from(c, 0)
        to_previous(c).wait()

        total = ret_1[c].astype(jnp.float32) + from_next[c].astype(jnp.float32)
        plus_out[:, :, cols(c)] = pltpu.einshape("erd->red", total.astype(jnp.bfloat16))

        @pl.loop(1, slabs)
        def _(k):
            give_back(c, k).wait()
            add_from(c, k)

        @pl.loop(0, cap)
        def _(slot):
            last = jnp.clip(last_sm[slot], 0, slabs * per_pair)
            owned_out[slot, :, cols(c)] = sums[last].astype(jnp.bfloat16)


def finish(a_in, b_in, c_in, a_out, b_out, c_out, sems):
    moves = [
        pltpu.make_async_copy(src, dst, sems.at[n])
        for n, (src, dst) in enumerate(((a_in, a_out), (b_in, b_out), (c_in, c_out)))
    ]
    for move in moves:
        move.start()
    for move in moves:
        move.wait()


def swap(array):
    return jnp.swapaxes(array, 0, 1)


def per_device(owned_trace, plus_trace, schur, recover, face_refs, orient):
    elems, trace = schur.shape[:2]
    dof, columns = plus_trace.shape[1:]
    inner = recover.shape[1]
    cap = owned_trace.shape[0]
    slabs, sectors = lax.axis_size("slab"), lax.axis_size("azim")
    per_pair = (4 * elems + slabs - 1) // slabs + 1
    width = columns // CHUNKS
    bf16, f32 = jnp.bfloat16, jnp.float32
    dma = pltpu.SemaphoreType.DMA
    arrivals = [
        pltpu.VMEM((slabs, per_pair, dof - (EARLY if c == 0 else 0), width), bf16) for c in range(CHUNKS)]
    exchange = pltpu.VMEM((CHUNKS, slabs, per_pair, dof, width), bf16)
    per_elem = pltpu.VMEM((CHUNKS, elems, dof, width), bf16)
    vmem = pl.BlockSpec(memory_space=pltpu.VMEM)
    hbm = pl.BlockSpec(memory_space=pltpu.HBM)
    outs = pl.pallas_call(
        functools.partial(kernel, (slabs, sectors, per_pair, elems, cap, dof, columns)),
        out_shape=(
            jax.ShapeDtypeStruct(owned_trace.shape, bf16),
            jax.ShapeDtypeStruct((dof, elems, columns), bf16),
            jax.ShapeDtypeStruct((inner, elems, columns), bf16),
        ),
        in_specs=[hbm] * 6,
        out_specs=(vmem, vmem, vmem),
        scratch_shapes=[
            pltpu.SMEM(face_refs.shape, jnp.int32),
            pltpu.SMEM(orient.shape, jnp.int32),
            pltpu.VMEM(owned_trace.shape, bf16),
            pltpu.VMEM((dof, elems, columns), bf16),
            pltpu.VMEM((dof, elems, columns), bf16),
            pltpu.VMEM((trace, elems, trace), bf16),
            pltpu.VMEM((inner, elems, trace), bf16),
            pltpu.VMEM(plus_trace.shape, bf16),
            pltpu.VMEM(plus_trace.shape, bf16),
            pltpu.VMEM(schur.shape, bf16),
            pltpu.VMEM(recover.shape, bf16),
            pltpu.VMEM((elems, inner, columns), bf16),
            pltpu.SMEM((slabs,) + face_refs.shape, jnp.int32),
            pltpu.SMEM((slabs * per_pair,), jnp.int32),
            pltpu.SMEM((slabs * per_pair,), jnp.int32),
            pltpu.SMEM((cap,), jnp.int32),
            pltpu.VMEM((8, 128), jnp.int32),
            pltpu.SMEM((8, 128), jnp.int32),
            pltpu.VMEM((elems, 6, dof, dof), bf16),
            pltpu.VMEM((elems, 6, dof, dof), bf16),
            arrivals, arrivals,
            pltpu.VMEM((slabs, cap, EARLY, width), bf16),
            pltpu.VMEM((dof, width), bf16),
            exchange, exchange,
            per_elem, per_elem,
            pltpu.VMEM((CHUNKS, 4 * elems, dof, width), bf16),
            per_elem,
            pltpu.VMEM((elems, trace, columns), bf16),
            pltpu.VMEM((trace, width), f32),
            pltpu.VMEM((trace, width), f32),
            pltpu.VMEM((slabs * per_pair + 1, dof, width), f32),
            dma((6,)), dma((slabs,)), dma((slabs,)), dma,
            dma((2,)), dma((slabs,)), dma((slabs,)),
            dma((CHUNKS, slabs)), dma((CHUNKS, slabs)),
            dma((CHUNKS, slabs)), dma((CHUNKS, slabs)),
            dma((CHUNKS,)), dma((CHUNKS,)), pltpu.SemaphoreType.REGULAR,
        ],
        compiler_params=pltpu.CompilerParams(
            collective_id=0, has_side_effects=True, vmem_limit_bytes=42 * 1024 * 1024),
    )(*(
        pltpu.with_memory_space_constraint(x, pltpu.HBM)
        for x in (face_refs, orient, owned_trace, swap(plus_trace), swap(schur), swap(recover))))
    owned_out, plus_out, inner_out = pl.pallas_call(
        finish,
        out_shape=tuple(jax.ShapeDtypeStruct(out.shape, out.dtype) for out in outs),
        in_specs=[vmem] * 3,
        out_specs=(hbm,) * 3,
        scratch_shapes=[dma((3,))],
        compiler_params=pltpu.CompilerParams(vmem_limit_bytes=1024 * 1024),
    )(*outs)
    return owned_out, swap(plus_out), swap(inner_out)


def solution(mesh):
    placed = P(("azim", "slab"), None, None)
    table = P(("azim", "slab"), None)
    return jax.shard_map(
        per_device,
        mesh=mesh,
        in_specs=(placed, placed, placed, placed, table, table),
        out_specs=(placed, placed, placed),
        check_vma=False,
    )
```

```python
import functools

import jax
import jax.numpy as jnp
from jax import lax
from jax.experimental import pallas as pl
from jax.experimental.pallas import tpu as pltpu
from jax.sharding import PartitionSpec as P

DEGREE = 4
CHUNKS = 2
EARLY = 16
ROWS = 144
MESH = pl.DeviceIdType.MESH


def source_of(face_row, code):
    side = DEGREE + 1
    variable = (face_row * 41) >> 10
    node = face_row - side * side * variable
    first = (node * 13) >> 6
    second = node - side * first
    swap, flip_first, flip_second = code & 1, (code >> 1) & 1, (code >> 2) & 1
    new_first = first + swap * (second - first)
    new_second = second + swap * (first - second)
    new_first = new_first + flip_first * (side - 1 - 2 * new_first)
    new_second = new_second + flip_second * (side - 1 - 2 * new_second)
    return side * side * variable + side * new_first + new_second


def in_blocks(rows, body):
    whole = rows // ROWS

    @pl.loop(0, whole)
    def _(b):
        body(pl.ds(pl.multiple_of(b * ROWS, ROWS), ROWS))

    if rows % ROWS:
        body(pl.ds(whole * ROWS, rows % ROWS))


def by_element(raw, out):
    def move(rows):
        out[:, rows, :] = pltpu.einshape("red->erd", raw[rows])

    in_blocks(raw.shape[0], move)


def partner(place, k, count):
    bit, other = 1, place
    while bit < count:
        other = other + ((k // bit) % 2) * bit * (1 - 2 * ((place // bit) % 2))
        bit *= 2
    return other


def kernel(
    dims,
    refs_hbm, orient_hbm, owned_hbm, plus_hbm, schur_hbm, recover_hbm,
    owned_out, plus_out, inner_out,
    refs_sm, orient_sm, owned_v, plus_raw, minus_raw, schur_raw, recover_raw,
    plus_v, minus_v, schur_v, recover_v, inner_v,
    asked_sm, slots_sm, before_sm, last_sm, req_v, req_sm, perm_v, permt_v,
    send_gs, recv_gs, early_v, face_v, send_r, recv_r,
    ret_0, ret_1, ret_k, from_next, local_v, local_32, resp_32, sums,
    load_sems, req_send, req_recv, table_sem,
    minus_sems, early_send, early_recv, gs_send, gs_recv, rt_send, rt_recv, fn_send, fn_recv, ready,
):
    slabs, sectors, per_pair, elems, cap, dof, columns = dims
    width = columns // CHUNKS
    ref_total = 4 * elems
    me_a, me_s = lax.axis_index("azim"), lax.axis_index("slab")
    next_a, prev_a = lax.rem(me_a + 1, sectors), lax.rem(me_a + sectors - 1, sectors)

    def peer(k):
        return (me_a, partner(me_s, k, slabs))

    loads = [
        pltpu.make_async_copy(src, dst, load_sems.at[n])
        for n, (src, dst) in enumerate(
            ((owned_hbm, owned_v), (plus_hbm, plus_raw), (schur_hbm, schur_raw), (recover_hbm, recover_raw),
             (refs_hbm, refs_sm), (orient_hbm, orient_sm))
        )
    ]

    barrier = pltpu.get_barrier_semaphore()

    @pl.loop(1, slabs)
    def _(k):
        pl.semaphore_signal(barrier, inc=1, device_id=peer(slabs - k), device_id_type=MESH)

    even = lax.rem(me_a, 2) == 0
    odd = jnp.logical_not(even)
    beside, across_a = jnp.where(even, next_a, prev_a), jnp.where(even, prev_a, next_a)
    first = across_a > me_a
    second = jnp.logical_not(first)
    pl.semaphore_signal(barrier, inc=1, device_id=(beside, me_s), device_id_type=MESH)

    @pl.when(first)
    def _():
        pl.semaphore_signal(barrier, inc=1, device_id=(across_a, me_s), device_id_type=MESH)

    for n in (0, 4):
        loads[n].start()

    def request(k):
        return pltpu.make_async_remote_copy(
            src_ref=refs_hbm, dst_ref=asked_sm.at[k], send_sem=req_send.at[k],
            recv_sem=req_recv.at[k], device_id=peer(k), device_id_type=MESH)

    minus = pltpu.make_async_remote_copy(
        src_ref=plus_hbm, dst_ref=minus_raw, send_sem=minus_sems.at[0],
        recv_sem=minus_sems.at[1], device_id=(next_a, me_s), device_id_type=MESH)

    @pl.when(first)
    def _():
        pl.semaphore_wait(barrier, slabs)

    @pl.when(second)
    def _():
        pl.semaphore_wait(barrier, slabs + 1)
        pl.semaphore_signal(ready, inc=1, device_id=(across_a, me_s), device_id_type=MESH)

    @pl.loop(1, slabs)
    def _(k):
        request(k).start()

    def early(k):
        return pltpu.make_async_remote_copy(
            src_ref=owned_hbm.at[:, pl.ds(0, EARLY), pl.ds(0, width)], dst_ref=early_v.at[k],
            send_sem=early_send.at[k], recv_sem=early_recv.at[k], device_id=peer(k), device_id_type=MESH)

    @pl.loop(1, slabs)
    def _(k):
        early(jnp.where(k == 1, slabs - 1, k - 1)).start()

    @pl.when(jnp.logical_or(even, second))
    def _():
        minus.start()

    for n in (5, 1, 2, 3):
        loads[n].start()

    def give(c, k):
        return pltpu.make_async_remote_copy(
            src_ref=send_gs[c].at[k], dst_ref=recv_gs[c].at[k], send_sem=gs_send.at[c, k],
            recv_sem=gs_recv.at[c, k], device_id=peer(k), device_id_type=MESH)

    def give_back(c, k):
        return pltpu.make_async_remote_copy(
            src_ref=send_r.at[c, k], dst_ref=recv_r.at[c, k], send_sem=rt_send.at[c, k],
            recv_sem=rt_recv.at[c, k], device_id=peer(k), device_id_type=MESH)

    def to_previous(c):
        return pltpu.make_async_remote_copy(
            src_ref=ret_0.at[c], dst_ref=from_next.at[c], send_sem=fn_send.at[c],
            recv_sem=fn_recv.at[c], device_id=(prev_a, me_s), device_id_type=MESH)

    def cols(c):
        return pl.ds(c * width, width)

    def first_row(c):
        return EARLY if c == 0 else 0

    def place_slot(k, read):
        slots = [jnp.int32(-1)] * per_pair
        count = jnp.int32(0)
        for i in range(ref_total):
            value = read(i) - me_s * cap
            mine = (value >= 0) & (value < cap)
            for q in range(min(i + 1, per_pair)):
                slots[q] = jnp.where(mine & (count == q), value, slots[q])
            count = count + mine.astype(jnp.int32)
        for q in range(per_pair):
            slots_sm[k * per_pair + q] = slots[q]

    def fill(c, k):
        for q in range(per_pair):
            slot = jnp.clip(slots_sm[k * per_pair + q], 0, cap - 1)
            send_gs[c][k, q] = owned_v[slot, pl.ds(first_row(c), dof - first_row(c)), cols(c)]
        give(c, k).start()

    loads[0].wait()

    @pl.loop(1, slabs)
    def _(k):
        request(k).wait()
        place_slot(k, lambda i: asked_sm[k, i // 4, i % 4])
        fill(0, k)

    for c in range(1, CHUNKS):
        @pl.loop(1, slabs)
        def _(k):
            fill(c, k)

    @pl.when(jnp.logical_and(odd, first))
    def _():
        pl.semaphore_wait(ready, 1)
        minus.start()

    early_v[0] = owned_v[:, pl.ds(0, EARLY), pl.ds(0, width)]
    loads[4].wait()
    place_slot(0, lambda i: refs_sm[i // 4, i % 4])
    for q in range(per_pair):
        slot = jnp.clip(slots_sm[q], 0, cap - 1)
        for c in range(CHUNKS):
            recv_gs[c][0, q] = owned_v[slot, pl.ds(first_row(c), dof - first_row(c)), cols(c)]

    @pl.loop(0, slabs * per_pair)
    def _(j):
        slot, before = slots_sm[j], jnp.int32(0)
        for i in range(slabs * per_pair):
            before = jnp.where((slots_sm[i] == slot) & (i < j), i + 1, before)
        before_sm[j] = before

    @pl.loop(0, cap)
    def _(slot):
        last = jnp.int32(0)
        for i in range(slabs * per_pair):
            last = jnp.where(slots_sm[i] == slot, i + 1, last)
        last_sm[slot] = last

    sub = lax.broadcasted_iota(jnp.int32, (ref_total, 128), 0)
    lane = lax.broadcasted_iota(jnp.int32, (ref_total, 128), 1)
    ref_c = jnp.zeros((ref_total, 128), jnp.int32)
    ref_r = jnp.full((ref_total, 128), slabs * cap, jnp.int32)
    for i in range(ref_total):
        value = refs_sm[i // 4, i % 4]
        ref_c = jnp.where(sub == i, value, ref_c)
        ref_r = jnp.where(lane == i, value, ref_r)
    owner_c = jnp.zeros((ref_total, 128), jnp.int32)
    owner_r = jnp.zeros((ref_total, 128), jnp.int32)
    for o in range(1, slabs + 1):
        owner_c = owner_c + (ref_c >= o * cap).astype(jnp.int32)
        owner_r = owner_r + (ref_r >= o * cap).astype(jnp.int32)
    ahead = jnp.where((owner_c == owner_r) & (lane < sub), 1.0, 0.0)
    rank = jnp.sum(ahead, axis=1, keepdims=True)
    shift = partner(owner_c, me_s, slabs)
    target = (shift * per_pair).astype(jnp.float32) + rank
    hit = target == lane.astype(jnp.float32)
    source = jnp.sum(jnp.where(hit, sub.astype(jnp.float32), 0.0), axis=0, keepdims=True)
    where_to = jnp.sum(jnp.where(lane == sub, target, 0.0), axis=0, keepdims=True)
    row = lax.broadcasted_iota(jnp.int32, (8, 128), 0)
    slot_of = jnp.sum(jnp.where(lane == sub, (ref_c - owner_c * cap).astype(jnp.float32), 0.0), axis=0, keepdims=True)
    req_v[...] = jnp.where(row == 0, source, jnp.where(row == 1, where_to, slot_of)).astype(jnp.int32)

    to_scalars = pltpu.make_async_copy(req_v, req_sm, table_sem)
    to_scalars.start()
    to_scalars.wait()

    loads[5].wait()
    down_rows = lax.broadcasted_iota(jnp.int32, (dof, dof), 0)
    across = lax.broadcasted_iota(jnp.int32, (dof, dof), 1)

    @pl.loop(0, elems)
    def _(e):
        for f in range(6):
            code = orient_sm[e, f]
            perm_v[e, f] = jnp.where(source_of(down_rows, code) == across, 1.0, 0.0).astype(jnp.bfloat16)
            permt_v[e, f] = jnp.where(source_of(across, code) == down_rows, 1.0, 0.0).astype(jnp.bfloat16)

    sums[0] = jnp.zeros_like(sums[0])
    loads[2].wait()
    by_element(schur_raw, schur_v)
    loads[1].wait()
    plus_v[...] = pltpu.einshape("red->erd", plus_raw[...])
    minus.wait()
    minus_v[...] = pltpu.einshape("red->erd", minus_raw[...])

    for c in range(CHUNKS):
        @pl.loop(1, slabs)
        def _(k):
            if c == 0:
                early(k).wait()
            give(c, k).wait()

        @pl.loop(0, elems)
        def _(e):
            for f in range(6):
                if f == 0:
                    face = minus_v[e, :, cols(c)]
                elif f == 1:
                    face = plus_v[e, :, cols(c)]
                else:
                    place = jnp.clip(req_sm[1, e * 4 + f - 2], 0, slabs * per_pair - 1)
                    if c == 0:
                        slot = jnp.clip(req_sm[2, e * 4 + f - 2], 0, cap - 1)
                        face_v[pl.ds(0, EARLY), :] = early_v[place // per_pair, slot]
                        face_v[pl.ds(EARLY, dof - EARLY), :] = recv_gs[c][place // per_pair, place % per_pair]
                        face = face_v[...]
                    else:
                        face = recv_gs[c][place // per_pair, place % per_pair]
                local_32[pl.ds(f * dof, dof), :] = jnp.dot(
                    perm_v[e, f], face, preferred_element_type=jnp.float32)
            local = local_32[...].astype(jnp.bfloat16)
            local_v[e, :, cols(c)] = local
            resp_32[...] = jnp.dot(schur_v[e], local, preferred_element_type=jnp.float32)
            for f in range(6):
                part = resp_32[pl.ds(f * dof, dof), :].astype(jnp.bfloat16)
                back = jnp.dot(permt_v[e, f], part, preferred_element_type=jnp.float32).astype(jnp.bfloat16)
                if f == 0:
                    ret_0[c, e] = back
                elif f == 1:
                    ret_1[c, e] = back
                else:
                    ret_k[c, e * 4 + f - 2] = back

        @pl.loop(1, slabs)
        def _(step):
            k = slabs - step
            for q in range(per_pair):
                origin = jnp.clip(req_sm[0, k * per_pair + q], 0, ref_total - 1)
                send_r[c, k, q] = ret_k[c, origin]
            give_back(c, k).start()

        if c == 0:
            @pl.when(jnp.logical_and(even, first))
            def _():
                pl.semaphore_wait(ready, 1)

        to_previous(c).start()
        for q in range(per_pair):
            origin = jnp.clip(req_sm[0, q], 0, ref_total - 1)
            recv_r[c, 0, q] = ret_k[c, origin]

    loads[3].wait()
    by_element(recover_raw, recover_v)

    @pl.loop(0, elems)
    def _(e):
        inner_v[e] = jnp.dot(recover_v[e], local_v[e], preferred_element_type=jnp.float32).astype(jnp.bfloat16)

    def interleave(rows):
        inner_out[rows] = pltpu.einshape("erd->red", inner_v[:, rows, :])

    in_blocks(inner_v.shape[1], interleave)

    def add_from(c, k):
        for q in range(per_pair):
            j = k * per_pair + q
            before = jnp.clip(before_sm[j], 0, slabs * per_pair)
            sums[j + 1] = recv_r[c, k, q].astype(jnp.float32) + sums[before]

    for c in range(CHUNKS):
        add_from(c, 0)
        to_previous(c).wait()

        total = ret_1[c].astype(jnp.float32) + from_next[c].astype(jnp.float32)
        plus_out[:, :, cols(c)] = pltpu.einshape("erd->red", total.astype(jnp.bfloat16))

        @pl.loop(1, slabs)
        def _(k):
            give_back(c, k).wait()
            add_from(c, k)

        @pl.loop(0, cap)
        def _(slot):
            last = jnp.clip(last_sm[slot], 0, slabs * per_pair)
            owned_out[slot, :, cols(c)] = sums[last].astype(jnp.bfloat16)


def finish(a_in, b_in, c_in, a_out, b_out, c_out, sems):
    moves = [
        pltpu.make_async_copy(src, dst, sems.at[n])
        for n, (src, dst) in enumerate(((a_in, a_out), (b_in, b_out), (c_in, c_out)))
    ]
    for move in moves:
        move.start()
    for move in moves:
        move.wait()


def swap(array):
    return jnp.swapaxes(array, 0, 1)


def per_device(owned_trace, plus_trace, schur, recover, face_refs, orient):
    elems, trace = schur.shape[:2]
    dof, columns = plus_trace.shape[1:]
    inner = recover.shape[1]
    cap = owned_trace.shape[0]
    slabs, sectors = lax.axis_size("slab"), lax.axis_size("azim")
    per_pair = (4 * elems + slabs - 1) // slabs + 1
    width = columns // CHUNKS
    bf16, f32 = jnp.bfloat16, jnp.float32
    dma = pltpu.SemaphoreType.DMA
    arrivals = [
        pltpu.VMEM((slabs, per_pair, dof - (EARLY if c == 0 else 0), width), bf16) for c in range(CHUNKS)]
    exchange = pltpu.VMEM((CHUNKS, slabs, per_pair, dof, width), bf16)
    per_elem = pltpu.VMEM((CHUNKS, elems, dof, width), bf16)
    vmem = pl.BlockSpec(memory_space=pltpu.VMEM)
    hbm = pl.BlockSpec(memory_space=pltpu.HBM)
    outs = pl.pallas_call(
        functools.partial(kernel, (slabs, sectors, per_pair, elems, cap, dof, columns)),
        out_shape=(
            jax.ShapeDtypeStruct(owned_trace.shape, bf16),
            jax.ShapeDtypeStruct((dof, elems, columns), bf16),
            jax.ShapeDtypeStruct((inner, elems, columns), bf16),
        ),
        in_specs=[hbm] * 6,
        out_specs=(vmem, vmem, vmem),
        scratch_shapes=[
            pltpu.SMEM(face_refs.shape, jnp.int32),
            pltpu.SMEM(orient.shape, jnp.int32),
            pltpu.VMEM(owned_trace.shape, bf16),
            pltpu.VMEM((dof, elems, columns), bf16),
            pltpu.VMEM((dof, elems, columns), bf16),
            pltpu.VMEM((trace, elems, trace), bf16),
            pltpu.VMEM((inner, elems, trace), bf16),
            pltpu.VMEM(plus_trace.shape, bf16),
            pltpu.VMEM(plus_trace.shape, bf16),
            pltpu.VMEM(schur.shape, bf16),
            pltpu.VMEM(recover.shape, bf16),
            pltpu.VMEM((elems, inner, columns), bf16),
            pltpu.SMEM((slabs,) + face_refs.shape, jnp.int32),
            pltpu.SMEM((slabs * per_pair,), jnp.int32),
            pltpu.SMEM((slabs * per_pair,), jnp.int32),
            pltpu.SMEM((cap,), jnp.int32),
            pltpu.VMEM((8, 128), jnp.int32),
            pltpu.SMEM((8, 128), jnp.int32),
            pltpu.VMEM((elems, 6, dof, dof), bf16),
            pltpu.VMEM((elems, 6, dof, dof), bf16),
            arrivals, arrivals,
            pltpu.VMEM((slabs, cap, EARLY, width), bf16),
            pltpu.VMEM((dof, width), bf16),
            exchange, exchange,
            per_elem, per_elem,
            pltpu.VMEM((CHUNKS, 4 * elems, dof, width), bf16),
            per_elem,
            pltpu.VMEM((elems, trace, columns), bf16),
            pltpu.VMEM((trace, width), f32),
            pltpu.VMEM((trace, width), f32),
            pltpu.VMEM((slabs * per_pair + 1, dof, width), f32),
            dma((6,)), dma((slabs,)), dma((slabs,)), dma,
            dma((2,)), dma((slabs,)), dma((slabs,)),
            dma((CHUNKS, slabs)), dma((CHUNKS, slabs)),
            dma((CHUNKS, slabs)), dma((CHUNKS, slabs)),
            dma((CHUNKS,)), dma((CHUNKS,)), pltpu.SemaphoreType.REGULAR,
        ],
        compiler_params=pltpu.CompilerParams(
            collective_id=0, has_side_effects=True, vmem_limit_bytes=42 * 1024 * 1024),
    )(*(
        pltpu.with_memory_space_constraint(x, pltpu.HBM)
        for x in (face_refs, orient, owned_trace, swap(plus_trace), swap(schur), swap(recover))))
    owned_out, plus_out, inner_out = pl.pallas_call(
        finish,
        out_shape=tuple(jax.ShapeDtypeStruct(out.shape, out.dtype) for out in outs),
        in_specs=[vmem] * 3,
        out_specs=(hbm,) * 3,
        scratch_shapes=[dma((3,))],
        compiler_params=pltpu.CompilerParams(vmem_limit_bytes=1024 * 1024),
    )(*outs)
    return owned_out, swap(plus_out), swap(inner_out)


def solution(mesh):
    placed = P(("azim", "slab"), None, None)
    table = P(("azim", "slab"), None)
    return jax.shard_map(
        per_device,
        mesh=mesh,
        in_specs=(placed, placed, placed, placed, table, table),
        out_specs=(placed, placed, placed),
        check_vma=False,
    )
```

```python
import functools

import jax
import jax.numpy as jnp
from jax import lax
from jax.experimental import pallas as pl
from jax.experimental.pallas import tpu as pltpu
from jax.sharding import PartitionSpec as P

DEGREE = 4
CHUNKS = 2
EARLY = 16
ROWS = 144
MESH = pl.DeviceIdType.MESH


def source_of(face_row, code):
    side = DEGREE + 1
    variable = (face_row * 41) >> 10
    node = face_row - side * side * variable
    first = (node * 13) >> 6
    second = node - side * first
    swap, flip_first, flip_second = code & 1, (code >> 1) & 1, (code >> 2) & 1
    new_first = first + swap * (second - first)
    new_second = second + swap * (first - second)
    new_first = new_first + flip_first * (side - 1 - 2 * new_first)
    new_second = new_second + flip_second * (side - 1 - 2 * new_second)
    return side * side * variable + side * new_first + new_second


def in_blocks(rows, body):
    whole = rows // ROWS

    @pl.loop(0, whole)
    def _(b):
        body(pl.ds(pl.multiple_of(b * ROWS, ROWS), ROWS))

    if rows % ROWS:
        body(pl.ds(whole * ROWS, rows % ROWS))


def by_element(raw, out):
    def move(rows):
        out[:, rows, :] = pltpu.einshape("red->erd", raw[rows])

    in_blocks(raw.shape[0], move)


def partner(place, k, count):
    bit, other = 1, place
    while bit < count:
        other = other + ((k // bit) % 2) * bit * (1 - 2 * ((place // bit) % 2))
        bit *= 2
    return other


def kernel(
    dims,
    refs_hbm, orient_hbm, owned_hbm, plus_hbm, schur_hbm, recover_hbm,
    owned_out, plus_out, inner_out,
    refs_sm, orient_sm, owned_v, plus_raw, minus_raw, schur_raw, recover_raw,
    plus_v, minus_v, schur_v, recover_v, inner_v,
    asked_sm, slots_sm, before_sm, last_sm, req_v, req_sm, perm_v, permt_v,
    send_gs, recv_gs, early_v, face_v, send_r, recv_r,
    ret_0, ret_1, ret_k, from_next, local_v, local_32, resp_32, sums,
    load_sems, req_send, req_recv, table_sem,
    minus_sems, early_send, early_recv, gs_send, gs_recv, rt_send, rt_recv, fn_send, fn_recv, ready,
):
    slabs, sectors, per_pair, elems, cap, dof, columns = dims
    width = columns // CHUNKS
    ref_total = 4 * elems
    me_a, me_s = lax.axis_index("azim"), lax.axis_index("slab")
    next_a, prev_a = lax.rem(me_a + 1, sectors), lax.rem(me_a + sectors - 1, sectors)

    def peer(k):
        return (me_a, partner(me_s, k, slabs))

    loads = [
        pltpu.make_async_copy(src, dst, load_sems.at[n])
        for n, (src, dst) in enumerate(
            ((owned_hbm, owned_v), (plus_hbm, plus_raw), (schur_hbm, schur_raw), (recover_hbm, recover_raw),
             (refs_hbm, refs_sm), (orient_hbm, orient_sm))
        )
    ]

    barrier = pltpu.get_barrier_semaphore()

    @pl.loop(1, slabs)
    def _(k):
        pl.semaphore_signal(barrier, inc=1, device_id=peer(slabs - k), device_id_type=MESH)

    even = lax.rem(me_a, 2) == 0
    odd = jnp.logical_not(even)
    beside, across_a = jnp.where(even, next_a, prev_a), jnp.where(even, prev_a, next_a)
    first = across_a > me_a
    second = jnp.logical_not(first)
    pl.semaphore_signal(barrier, inc=1, device_id=(beside, me_s), device_id_type=MESH)

    @pl.when(first)
    def _():
        pl.semaphore_signal(barrier, inc=1, device_id=(across_a, me_s), device_id_type=MESH)

    for n in (0, 4):
        loads[n].start()

    def request(k):
        return pltpu.make_async_remote_copy(
            src_ref=refs_hbm, dst_ref=asked_sm.at[k], send_sem=req_send.at[k],
            recv_sem=req_recv.at[k], device_id=peer(k), device_id_type=MESH)

    minus = pltpu.make_async_remote_copy(
        src_ref=plus_hbm, dst_ref=minus_raw, send_sem=minus_sems.at[0],
        recv_sem=minus_sems.at[1], device_id=(next_a, me_s), device_id_type=MESH)

    @pl.when(first)
    def _():
        pl.semaphore_wait(barrier, slabs)

    @pl.when(second)
    def _():
        pl.semaphore_wait(barrier, slabs + 1)
        pl.semaphore_signal(ready, inc=1, device_id=(across_a, me_s), device_id_type=MESH)

    @pl.loop(1, slabs)
    def _(k):
        request(k).start()

    def early(k):
        return pltpu.make_async_remote_copy(
            src_ref=owned_hbm.at[:, pl.ds(0, EARLY), pl.ds(0, width)], dst_ref=early_v.at[k],
            send_sem=early_send.at[k], recv_sem=early_recv.at[k], device_id=peer(k), device_id_type=MESH)

    @pl.loop(1, slabs)
    def _(k):
        early(jnp.where(k == 1, slabs - 1, k - 1)).start()

    for n in (5, 1, 2, 3):
        loads[n].start()

    def give(c, k):
        return pltpu.make_async_remote_copy(
            src_ref=send_gs[c].at[k], dst_ref=recv_gs[c].at[k], send_sem=gs_send.at[c, k],
            recv_sem=gs_recv.at[c, k], device_id=peer(k), device_id_type=MESH)

    def give_back(c, k):
        return pltpu.make_async_remote_copy(
            src_ref=send_r.at[c, k], dst_ref=recv_r.at[c, k], send_sem=rt_send.at[c, k],
            recv_sem=rt_recv.at[c, k], device_id=peer(k), device_id_type=MESH)

    def to_previous(c):
        return pltpu.make_async_remote_copy(
            src_ref=ret_0.at[c], dst_ref=from_next.at[c], send_sem=fn_send.at[c],
            recv_sem=fn_recv.at[c], device_id=(prev_a, me_s), device_id_type=MESH)

    def cols(c):
        return pl.ds(c * width, width)

    def first_row(c):
        return EARLY if c == 0 else 0

    def place_slot(k, read):
        slots = [jnp.int32(-1)] * per_pair
        count = jnp.int32(0)
        for i in range(ref_total):
            value = read(i) - me_s * cap
            mine = (value >= 0) & (value < cap)
            for q in range(min(i + 1, per_pair)):
                slots[q] = jnp.where(mine & (count == q), value, slots[q])
            count = count + mine.astype(jnp.int32)
        for q in range(per_pair):
            slots_sm[k * per_pair + q] = slots[q]

    def fill(c, k):
        for q in range(per_pair):
            slot = jnp.clip(slots_sm[k * per_pair + q], 0, cap - 1)
            send_gs[c][k, q] = owned_v[slot, pl.ds(first_row(c), dof - first_row(c)), cols(c)]
        give(c, k).start()

    loads[0].wait()

    @pl.loop(1, slabs)
    def _(k):
        request(k).wait()
        place_slot(k, lambda i: asked_sm[k, i // 4, i % 4])
        fill(0, k)

    for c in range(1, CHUNKS):
        @pl.loop(1, slabs)
        def _(k):
            fill(c, k)

    @pl.when(jnp.logical_and(odd, first))
    def _():
        pl.semaphore_wait(ready, 1)

    minus.start()

    early_v[0] = owned_v[:, pl.ds(0, EARLY), pl.ds(0, width)]
    loads[4].wait()
    place_slot(0, lambda i: refs_sm[i // 4, i % 4])
    for q in range(per_pair):
        slot = jnp.clip(slots_sm[q], 0, cap - 1)
        for c in range(CHUNKS):
            recv_gs[c][0, q] = owned_v[slot, pl.ds(first_row(c), dof - first_row(c)), cols(c)]

    @pl.loop(0, slabs * per_pair)
    def _(j):
        slot, before = slots_sm[j], jnp.int32(0)
        for i in range(slabs * per_pair):
            before = jnp.where((slots_sm[i] == slot) & (i < j), i + 1, before)
        before_sm[j] = before

    @pl.loop(0, cap)
    def _(slot):
        last = jnp.int32(0)
        for i in range(slabs * per_pair):
            last = jnp.where(slots_sm[i] == slot, i + 1, last)
        last_sm[slot] = last

    sub = lax.broadcasted_iota(jnp.int32, (ref_total, 128), 0)
    lane = lax.broadcasted_iota(jnp.int32, (ref_total, 128), 1)
    ref_c = jnp.zeros((ref_total, 128), jnp.int32)
    ref_r = jnp.full((ref_total, 128), slabs * cap, jnp.int32)
    for i in range(ref_total):
        value = refs_sm[i // 4, i % 4]
        ref_c = jnp.where(sub == i, value, ref_c)
        ref_r = jnp.where(lane == i, value, ref_r)
    owner_c = jnp.zeros((ref_total, 128), jnp.int32)
    owner_r = jnp.zeros((ref_total, 128), jnp.int32)
    for o in range(1, slabs + 1):
        owner_c = owner_c + (ref_c >= o * cap).astype(jnp.int32)
        owner_r = owner_r + (ref_r >= o * cap).astype(jnp.int32)
    ahead = jnp.where((owner_c == owner_r) & (lane < sub), 1.0, 0.0)
    rank = jnp.sum(ahead, axis=1, keepdims=True)
    shift = partner(owner_c, me_s, slabs)
    target = (shift * per_pair).astype(jnp.float32) + rank
    hit = target == lane.astype(jnp.float32)
    source = jnp.sum(jnp.where(hit, sub.astype(jnp.float32), 0.0), axis=0, keepdims=True)
    where_to = jnp.sum(jnp.where(lane == sub, target, 0.0), axis=0, keepdims=True)
    row = lax.broadcasted_iota(jnp.int32, (8, 128), 0)
    slot_of = jnp.sum(jnp.where(lane == sub, (ref_c - owner_c * cap).astype(jnp.float32), 0.0), axis=0, keepdims=True)
    req_v[...] = jnp.where(row == 0, source, jnp.where(row == 1, where_to, slot_of)).astype(jnp.int32)

    to_scalars = pltpu.make_async_copy(req_v, req_sm, table_sem)
    to_scalars.start()
    to_scalars.wait()

    loads[5].wait()
    down_rows = lax.broadcasted_iota(jnp.int32, (dof, dof), 0)
    across = lax.broadcasted_iota(jnp.int32, (dof, dof), 1)

    @pl.loop(0, elems)
    def _(e):
        for f in range(6):
            code = orient_sm[e, f]
            perm_v[e, f] = jnp.where(source_of(down_rows, code) == across, 1.0, 0.0).astype(jnp.bfloat16)
            permt_v[e, f] = jnp.where(source_of(across, code) == down_rows, 1.0, 0.0).astype(jnp.bfloat16)

    sums[0] = jnp.zeros_like(sums[0])
    loads[2].wait()
    by_element(schur_raw, schur_v)
    loads[1].wait()
    plus_v[...] = pltpu.einshape("red->erd", plus_raw[...])
    minus.wait()
    minus_v[...] = pltpu.einshape("red->erd", minus_raw[...])

    for c in range(CHUNKS):
        @pl.loop(1, slabs)
        def _(k):
            if c == 0:
                early(k).wait()
            give(c, k).wait()

        @pl.loop(0, elems)
        def _(e):
            for f in range(6):
                if f == 0:
                    face = minus_v[e, :, cols(c)]
                elif f == 1:
                    face = plus_v[e, :, cols(c)]
                else:
                    place = jnp.clip(req_sm[1, e * 4 + f - 2], 0, slabs * per_pair - 1)
                    if c == 0:
                        slot = jnp.clip(req_sm[2, e * 4 + f - 2], 0, cap - 1)
                        face_v[pl.ds(0, EARLY), :] = early_v[place // per_pair, slot]
                        face_v[pl.ds(EARLY, dof - EARLY), :] = recv_gs[c][place // per_pair, place % per_pair]
                        face = face_v[...]
                    else:
                        face = recv_gs[c][place // per_pair, place % per_pair]
                local_32[pl.ds(f * dof, dof), :] = jnp.dot(
                    perm_v[e, f], face, preferred_element_type=jnp.float32)
            local = local_32[...].astype(jnp.bfloat16)
            local_v[e, :, cols(c)] = local
            resp_32[...] = jnp.dot(schur_v[e], local, preferred_element_type=jnp.float32)
            for f in range(6):
                part = resp_32[pl.ds(f * dof, dof), :].astype(jnp.bfloat16)
                back = jnp.dot(permt_v[e, f], part, preferred_element_type=jnp.float32).astype(jnp.bfloat16)
                if f == 0:
                    ret_0[c, e] = back
                elif f == 1:
                    ret_1[c, e] = back
                else:
                    ret_k[c, e * 4 + f - 2] = back

        @pl.loop(1, slabs)
        def _(step):
            k = slabs - step
            for q in range(per_pair):
                origin = jnp.clip(req_sm[0, k * per_pair + q], 0, ref_total - 1)
                send_r[c, k, q] = ret_k[c, origin]
            give_back(c, k).start()

        if c == 0:
            @pl.when(jnp.logical_and(even, first))
            def _():
                pl.semaphore_wait(ready, 1)

        to_previous(c).start()
        for q in range(per_pair):
            origin = jnp.clip(req_sm[0, q], 0, ref_total - 1)
            recv_r[c, 0, q] = ret_k[c, origin]

    loads[3].wait()
    by_element(recover_raw, recover_v)

    @pl.loop(0, elems)
    def _(e):
        inner_v[e] = jnp.dot(recover_v[e], local_v[e], preferred_element_type=jnp.float32).astype(jnp.bfloat16)

    def interleave(rows):
        inner_out[rows] = pltpu.einshape("erd->red", inner_v[:, rows, :])

    in_blocks(inner_v.shape[1], interleave)

    def add_from(c, k):
        for q in range(per_pair):
            j = k * per_pair + q
            before = jnp.clip(before_sm[j], 0, slabs * per_pair)
            sums[j + 1] = recv_r[c, k, q].astype(jnp.float32) + sums[before]

    @pl.loop(0, CHUNKS)
    def _(c):
        here = pl.ds(pl.multiple_of(c * width, width), width)
        add_from(c, 0)
        to_previous(c).wait()
        total = ret_1[c].astype(jnp.float32) + from_next[c].astype(jnp.float32)
        plus_out[:, :, here] = pltpu.einshape("erd->red", total.astype(jnp.bfloat16))

        @pl.loop(1, slabs)
        def _(k):
            give_back(c, k).wait()
            add_from(c, k)

        @pl.loop(0, cap)
        def _(slot):
            last = jnp.clip(last_sm[slot], 0, slabs * per_pair)
            owned_out[slot, :, here] = sums[last].astype(jnp.bfloat16)


def finish(a_in, b_in, c_in, a_out, b_out, c_out, sems):
    moves = [
        pltpu.make_async_copy(src, dst, sems.at[n])
        for n, (src, dst) in enumerate(((a_in, a_out), (b_in, b_out), (c_in, c_out)))
    ]
    for move in moves:
        move.start()
    for move in moves:
        move.wait()


def swap(array):
    return jnp.swapaxes(array, 0, 1)


def per_device(owned_trace, plus_trace, schur, recover, face_refs, orient):
    elems, trace = schur.shape[:2]
    dof, columns = plus_trace.shape[1:]
    inner = recover.shape[1]
    cap = owned_trace.shape[0]
    slabs, sectors = lax.axis_size("slab"), lax.axis_size("azim")
    per_pair = (4 * elems + slabs - 1) // slabs + 1
    width = columns // CHUNKS
    bf16, f32 = jnp.bfloat16, jnp.float32
    dma = pltpu.SemaphoreType.DMA
    arrivals = [
        pltpu.VMEM((slabs, per_pair, dof - (EARLY if c == 0 else 0), width), bf16) for c in range(CHUNKS)]
    exchange = pltpu.VMEM((CHUNKS, slabs, per_pair, dof, width), bf16)
    per_elem = pltpu.VMEM((CHUNKS, elems, dof, width), bf16)
    vmem = pl.BlockSpec(memory_space=pltpu.VMEM)
    hbm = pl.BlockSpec(memory_space=pltpu.HBM)
    outs = pl.pallas_call(
        functools.partial(kernel, (slabs, sectors, per_pair, elems, cap, dof, columns)),
        out_shape=(
            jax.ShapeDtypeStruct(owned_trace.shape, bf16),
            jax.ShapeDtypeStruct((dof, elems, columns), bf16),
            jax.ShapeDtypeStruct((inner, elems, columns), bf16),
        ),
        in_specs=[hbm] * 6,
        out_specs=(vmem, vmem, vmem),
        scratch_shapes=[
            pltpu.SMEM(face_refs.shape, jnp.int32),
            pltpu.SMEM(orient.shape, jnp.int32),
            pltpu.VMEM(owned_trace.shape, bf16),
            pltpu.VMEM((dof, elems, columns), bf16),
            pltpu.VMEM((dof, elems, columns), bf16),
            pltpu.VMEM((trace, elems, trace), bf16),
            pltpu.VMEM((inner, elems, trace), bf16),
            pltpu.VMEM(plus_trace.shape, bf16),
            pltpu.VMEM(plus_trace.shape, bf16),
            pltpu.VMEM(schur.shape, bf16),
            pltpu.VMEM(recover.shape, bf16),
            pltpu.VMEM((elems, inner, columns), bf16),
            pltpu.SMEM((slabs,) + face_refs.shape, jnp.int32),
            pltpu.SMEM((slabs * per_pair,), jnp.int32),
            pltpu.SMEM((slabs * per_pair,), jnp.int32),
            pltpu.SMEM((cap,), jnp.int32),
            pltpu.VMEM((8, 128), jnp.int32),
            pltpu.SMEM((8, 128), jnp.int32),
            pltpu.VMEM((elems, 6, dof, dof), bf16),
            pltpu.VMEM((elems, 6, dof, dof), bf16),
            arrivals, arrivals,
            pltpu.VMEM((slabs, cap, EARLY, width), bf16),
            pltpu.VMEM((dof, width), bf16),
            exchange, exchange,
            per_elem, per_elem,
            pltpu.VMEM((CHUNKS, 4 * elems, dof, width), bf16),
            per_elem,
            pltpu.VMEM((elems, trace, columns), bf16),
            pltpu.VMEM((trace, width), f32),
            pltpu.VMEM((trace, width), f32),
            pltpu.VMEM((slabs * per_pair + 1, dof, width), f32),
            dma((6,)), dma((slabs,)), dma((slabs,)), dma,
            dma((2,)), dma((slabs,)), dma((slabs,)),
            dma((CHUNKS, slabs)), dma((CHUNKS, slabs)),
            dma((CHUNKS, slabs)), dma((CHUNKS, slabs)),
            dma((CHUNKS,)), dma((CHUNKS,)), pltpu.SemaphoreType.REGULAR,
        ],
        compiler_params=pltpu.CompilerParams(
            collective_id=0, has_side_effects=True, vmem_limit_bytes=42 * 1024 * 1024),
    )(*(
        pltpu.with_memory_space_constraint(x, pltpu.HBM)
        for x in (face_refs, orient, owned_trace, swap(plus_trace), swap(schur), swap(recover))))
    owned_out, plus_out, inner_out = pl.pallas_call(
        finish,
        out_shape=tuple(jax.ShapeDtypeStruct(out.shape, out.dtype) for out in outs),
        in_specs=[vmem] * 3,
        out_specs=(hbm,) * 3,
        scratch_shapes=[dma((3,))],
        compiler_params=pltpu.CompilerParams(vmem_limit_bytes=1024 * 1024),
    )(*outs)
    return owned_out, swap(plus_out), swap(inner_out)


def solution(mesh):
    placed = P(("azim", "slab"), None, None)
    table = P(("azim", "slab"), None)
    return jax.shard_map(
        per_device,
        mesh=mesh,
        in_specs=(placed, placed, placed, placed, table, table),
        out_specs=(placed, placed, placed),
        check_vma=False,
    )
```
